512 devices in a mesh: gz: 16 (over z), xy: 32 (over x, y, core).
Axes of the slice: x: 4, y: 4, z: 16, core: 2. Of those that a mesh axis runs over, the one named last changes fastest.
Arguments:
- source: float32 [512, 128, 512], P('gz', 'xy'), may hold values from -6 to 6
- potential: float32 [512, 128, 512], P('gz', 'xy'), may hold values from -6 to 6
Outputs:
- new_potential: float32 [512, 128, 512], P('gz', 'xy')
The draws below stay inside these ranges and needn't reach their ends.
All inputs are finite; a program needn't handle non-finite values.
Results may differ from the reference program's by a relative error of at most 0.0003.
Values sent between devices are 32-bit elements; how exact they have to be, the bound alone decides.
A program may use at most 64 MiB of HBM per device.

```python
import math
import jax
import jax.numpy as jnp
from jax import lax

NY = 512
SWEEPS = 2
SCREEN = 64
NZ = 512
NX = 128


def draw_source(key, part):
    return jnp.clip(jax.random.normal(key, (NZ, NX, NY), jnp.float32), -6.0, 6.0)


def level_of(stream_key, extent, cuts, least, top_value):
    factor_of, own = 1.0, jax.random.fold_in(stream_key, 6)
    for position, parts in cuts:
        steps = jnp.exp(jax.random.uniform(jax.random.fold_in(own, position), (parts,), jnp.float32, least / len(cuts), top_value / len(cuts)))
        factor_of = factor_of * jnp.repeat(steps, extent[position] // parts).reshape([-1 if axis == position else 1 for axis in range(len(extent))])
    return factor_of


def bell_draw(rng, shape, width, reach, cuts=(), held_as=jnp.bfloat16):
    level = level_of(rng, shape, cuts, -0.22, 0.18) if cuts else 1.0
    drawn = jax.random.normal(rng, shape, jnp.float32) * width * level
    return jnp.minimum(jnp.maximum(drawn, -reach), reach).astype(held_as)


def setup_inputs(seed: int = 0) -> dict:
    streams_of = jax.random.split(jax.random.key(seed), 3)
    source = draw_source(jax.random.fold_in(streams_of[2], 71), 0)
    potential = bell_draw(streams_of[1], (NZ, NX, NY), 1.0, 6.0, ((0, 16), (1, 32)), jnp.float32)
    return dict(source=source, potential=potential)


OMEGA = 0.8
HIGH = lax.Precision.HIGHEST

def sine_table(count):
    idx = jnp.arange(1, count + 1, dtype=jnp.int32)
    turns = idx[:, None] * idx[None, :] % (2 * (count + 1))
    return math.sqrt(2.0 / (count + 1)) * jnp.sin(math.pi / (count + 1) * turns.astype(jnp.float32))

def eigenvalues(count):
    idx = (jnp.arange(count, dtype=jnp.int32) + 1).astype(jnp.float32)
    return 2.0 - 2.0 * jnp.cos(math.pi / (count + 1) * idx)

def neighbours(field):
    padded = jnp.pad(field, 1)
    total = padded[2:, 1:-1, 1:-1] + padded[:-2, 1:-1, 1:-1]
    total = total + padded[1:-1, 2:, 1:-1] + padded[1:-1, :-2, 1:-1]
    total = total + padded[1:-1, 1:-1, 2:] + padded[1:-1, 1:-1, :-2]
    return total

def reference(source, potential):
    kappa = 1.0 / (SCREEN * SCREEN)
    centre_weight = 6.0 + kappa
    field = potential
    for sweep in range(SWEEPS):
        field = field + OMEGA * (source - (centre_weight * field - neighbours(field))) / centre_weight
    residual = source - (centre_weight * field - neighbours(field))
    nz, nx, ny = residual.shape
    mz, mx, my = (nz // 2, nx // 2, ny // 2)
    coarse = residual.reshape(mz, 2, mx, 2, my, 2).mean(axis=(1, 3, 5))
    table_z, table_x, table_y = (sine_table(mz), sine_table(mx), sine_table(my))
    spec = jnp.einsum('az,zxy->axy', table_z, coarse, precision=HIGH)
    spec = jnp.einsum('bx,axy->aby', table_x, spec, precision=HIGH)
    spec = jnp.einsum('cy,aby->abc', table_y, spec, precision=HIGH)
    denom = (eigenvalues(mz)[:, None, None] + eigenvalues(mx)[None, :, None] + eigenvalues(my)[None, None, :]) / 4.0 + kappa
    spec = spec / denom
    spec = jnp.einsum('az,axy->zxy', table_z, spec, precision=HIGH)
    spec = jnp.einsum('bx,zby->zxy', table_x, spec, precision=HIGH)
    correction = jnp.einsum('cy,zxc->zxy', table_y, spec, precision=HIGH)
    lifted = jnp.broadcast_to(correction[:, None, :, None, :, None], (mz, 2, mx, 2, my, 2)).reshape(nz, nx, ny)
    field = field + lifted
    for sweep in range(SWEEPS):
        field = field + OMEGA * (source - (centre_weight * field - neighbours(field))) / centre_weight
    return field
```

```python
import functools
import math

import jax
import jax.numpy as jnp
import numpy as np
from jax import lax
from jax.experimental import pallas as pl
from jax.experimental.pallas import tpu as pltpu
from jax.sharding import PartitionSpec as P

SCREEN = 64
OMEGA = 0.8
KAPPA = 1.0 / (SCREEN * SCREEN)
CW = 6.0 + KAPPA
HIGH = lax.Precision.HIGHEST
M = 8
CORNERS = ((-1, -1), (-1, 1), (1, -1), (1, 1))


def sine(count):
    idx = np.arange(1, count + 1, dtype=np.int64)
    turns = idx[:, None] * idx[None, :] % (2 * (count + 1))
    return math.sqrt(2.0 / (count + 1)) * np.sin(math.pi / (count + 1) * turns)


def eigen(count):
    return 2.0 - 2.0 * np.cos(math.pi / (count + 1) * np.arange(1, count + 1))


def tables(groups):
    nx, ny = 2 * groups, M * groups
    sx, sy = sine(nx), sine(ny)
    ty = np.repeat(sy, 2, axis=1)
    order = np.concatenate([np.arange(0, nx, 2), np.arange(1, nx, 2)])
    fx = 0.5 * np.concatenate([sx[order], sx[order]], axis=1)
    bx = np.zeros((groups, 8, 2 * nx))
    for d in range(groups):
        for e in range(4):
            x = 2 * d - 1 + e
            if 0 <= x < nx:
                bx[d, e, :nx] = sx[x]
                bx[d, 4 + e, nx:] = sx[x]
    diag = 2.0 + eigen(nx)[None, None, :] + eigen(ny).reshape(M, groups).T[:, :, None] + 4.0 * KAPPA
    theta = np.arccosh(0.5 * diag)
    theta = np.concatenate([theta, theta], axis=2)
    f = lambda t: np.asarray(t, np.float32)
    return f(ty), f(fx), f(bx.reshape(groups * 8, 2 * nx)), f(theta)


def kernel(
    gz, xy, src_hbm, pot_hbm, ty_hbm, fx_hbm, bx_hbm, th_hbm, out_ref,
    potv, srcv, ty, fx, bx, th, pa, pb, sv,
    xps, xpr, xss, xsr, zpr, zsr, cs, cr,
    xqs, xqr, zqr, ds, dr,
    rs, s1, r1, fz, wz, ztile, zr, vz, s2, r2, cc,
    ld, e1s, e1r, e2s, e2r, a1s, a1r, gs, gr, a2s, a2r,
):
    q, me = lax.axis_index("gz"), lax.axis_index("xy")
    planes, rows, ny = potv.shape
    half = 2 * xy

    loads = [
        pltpu.make_async_copy(pot_hbm, potv, ld.at[0]),
        pltpu.make_async_copy(src_hbm, srcv, ld.at[1]),
        pltpu.make_async_copy(ty_hbm, ty, ld.at[2]),
        pltpu.make_async_copy(fx_hbm, fx, ld.at[3]),
        pltpu.make_async_copy(bx_hbm, bx, ld.at[4]),
        pltpu.make_async_copy(th_hbm.at[me], th, ld.at[5]),
    ]
    for copy in loads:
        copy.start()

    def shifted(dz, dx):
        where = {}
        if dz:
            where["gz"] = lax.rem(q + dz + gz, gz)
        if dx:
            where["xy"] = lax.rem(me + dx + xy, xy)
        return where

    barrier = pltpu.get_barrier_semaphore()
    for dz, dx in CORNERS:
        pl.semaphore_signal(barrier, inc=1, device_id=shifted(dz, dx), device_id_type=pl.DeviceIdType.MESH)

    def greet_x(i, carry):
        pl.semaphore_signal(barrier, inc=1, device_id={"xy": lax.rem(me + i, xy)}, device_id_type=pl.DeviceIdType.MESH)
        return carry

    def greet_z(i, carry):
        pl.semaphore_signal(barrier, inc=1, device_id={"gz": lax.rem(q + i, gz)}, device_id_type=pl.DeviceIdType.MESH)
        return carry

    lax.fori_loop(1, xy, greet_x, 0)
    lax.fori_loop(1, gz, greet_z, 0)

    pa[...] = jnp.zeros_like(pa)
    sv[...] = jnp.zeros_like(sv)
    loads[0].wait()
    loads[1].wait()
    xps[0] = potv[:, 0:2, :]
    xps[1] = potv[:, 2:4, :]
    xss[0] = srcv[:, 0:1, :]
    xss[1] = srcv[:, 3:4, :]
    for c, (dz, dx) in enumerate(CORNERS):
        z, x = 0 if dz < 0 else planes - 1, 0 if dx < 0 else rows - 1
        cs[c] = potv[z, x : x + 1, :]
    pl.semaphore_wait(barrier, (xy - 1) + (gz - 1) + len(CORNERS))

    def remote(src, dst, send, recv, where):
        return pltpu.make_async_remote_copy(
            src_ref=src, dst_ref=dst, send_sem=send, recv_sem=recv,
            device_id=where, device_id_type=pl.DeviceIdType.MESH,
        )

    first = []
    for side, step in ((0, -1), (1, 1)):
        z = 0 if step < 0 else planes - 2
        z1 = 0 if step < 0 else planes - 1
        first.append(remote(xps.at[side], xpr.at[side], e1s.at[side], e1r.at[side], shifted(0, step)))
        first.append(remote(xss.at[side], xsr.at[side], e1s.at[2 + side], e1r.at[2 + side], shifted(0, step)))
        first.append(remote(potv.at[pl.ds(z, 2)], zpr.at[side], e1s.at[4 + side], e1r.at[4 + side], shifted(step, 0)))
        first.append(remote(srcv.at[pl.ds(z1, 1)], zsr.at[side], e1s.at[6 + side], e1r.at[6 + side], shifted(step, 0)))
    for c, (dz, dx) in enumerate(CORNERS):
        first.append(remote(cs.at[c], cr.at[c], e1s.at[8 + c], e1r.at[8 + c], shifted(dz, dx)))
    for copy in first:
        copy.start()

    pa[2 : planes + 2, 2:6, :] = potv[...]
    sv[1 : planes + 1, 2:6, :] = srcv[...]
    sub = lax.broadcasted_iota(jnp.int32, (8, ny), 0)
    lane = lax.broadcasted_iota(jnp.int32, (8, ny), 1)
    inside = jnp.logical_and(
        jnp.logical_or(sub >= 2, me > 0), jnp.logical_or(sub < 6, me < xy - 1)
    )
    low, high = (q > 0).astype(jnp.float32), (q < gz - 1).astype(jnp.float32)
    near, far = (me > 0).astype(jnp.float32), (me < xy - 1).astype(jnp.float32)

    def corners_in(corner):
        for c, (dz, dx) in enumerate(CORNERS):
            plane, edge = (planes + 2, high) if dz < 0 else (1, low)
            row, side = (6, far) if dx < 0 else (1, near)
            pa[plane, row : row + 1, :] = corner[c] * (edge * side)

    for copy in first:
        copy.wait()
    pa[2 : planes + 2, 0:2, :] = xpr[1] * near
    pa[2 : planes + 2, 6:8, :] = xpr[0] * far
    pa[0:2, 2:6, :] = zpr[1] * low
    pa[planes + 2 : planes + 4, 2:6, :] = zpr[0] * high
    sv[1 : planes + 1, 1:2, :] = xsr[1] * near
    sv[1 : planes + 1, 6:7, :] = xsr[0] * far
    sv[0:1, 2:6, :] = zsr[1] * low
    sv[planes + 1 : planes + 2, 2:6, :] = zsr[0] * high
    corners_in(cr)

    def neighbours(ref, i):
        v = ref[i]
        total = ref[i - 1] + ref[i + 1]
        total = total + pltpu.roll(v, 1, 0) + pltpu.roll(v, 7, 0)
        total = total + jnp.where(lane == 0, 0.0, pltpu.roll(v, 1, 1))
        total = total + jnp.where(lane == ny - 1, 0.0, pltpu.roll(v, ny - 1, 1))
        return v, total

    def relax(ref, i):
        v, total = neighbours(ref, i)
        return (1.0 - OMEGA) * v + (OMEGA / CW) * (sv[i - 1] + total)

    def wide_sweep():
        def step(i, carry):
            pb[i] = jnp.where(inside, relax(pa, i), 0.0)
            return carry

        lax.fori_loop(1, planes + 3, step, 0, unroll=2)
        pb[1] = pb[1] * low
        pb[planes + 2] = pb[planes + 2] * high

    wide_sweep()

    def own_sweep(i, carry):
        pa[i] = relax(pb, i)
        return carry

    lax.fori_loop(2, planes + 2, own_sweep, 0, unroll=2)

    xqs[0] = pa[2 : planes + 2, 2:4, :]
    xqs[1] = pa[2 : planes + 2, 4:6, :]
    for c, (dz, dx) in enumerate(CORNERS):
        z, x = 2 if dz < 0 else planes + 1, 2 if dx < 0 else 5
        ds[c] = pa[z, x : x + 1, :]
    second = []
    for side, step in ((0, -1), (1, 1)):
        z = 2 if step < 0 else planes
        second.append(remote(xqs.at[side], xqr.at[side], e2s.at[side], e2r.at[side], shifted(0, step)))
        second.append(remote(pa.at[pl.ds(z, 2)], zqr.at[side], e2s.at[2 + side], e2r.at[2 + side], shifted(step, 0)))
    for c, (dz, dx) in enumerate(CORNERS):
        second.append(remote(ds.at[c], dr.at[c], e2s.at[4 + c], e2r.at[4 + c], shifted(dz, dx)))
    for copy in second:
        copy.start()
    for copy in second:
        copy.wait()
    pa[2 : planes + 2, 0:2, :] = xqr[1] * near
    pa[2 : planes + 2, 6:8, :] = xqr[0] * far
    pa[0:2, 2:6, :] = zqr[1, :, 2:6, :] * low
    pa[planes + 2 : planes + 4, 2:6, :] = zqr[0, :, 2:6, :] * high
    corners_in(dr)

    def residual(i):
        v, total = neighbours(pa, i)
        return sv[i - 1] - CW * v + total

    def coarsen(z, carry):
        rs[z] = residual(2 * z + 2) + residual(2 * z + 3)
        return carry

    coarse = planes // 2
    lax.fori_loop(0, coarse, coarsen, 0)
    for copy in loads[2:]:
        copy.wait()
    wide = coarse * 8
    spec = lax.dot_general(
        ty[...], rs[...].reshape(wide, ny), (((1,), (1,)), ((), ())),
        precision=HIGH, preferred_element_type=jnp.float32,
    )
    spec = spec + pltpu.roll(spec, wide - 1, 1)
    slot = lax.broadcasted_iota(jnp.int32, (xy, wide), 1) % 8
    for xx in range(2):
        packed = jnp.zeros((xy, wide), jnp.float32)
        for m in range(M):
            piece = spec[m * xy : (m + 1) * xy, :]
            shift = (m - 2 - 2 * xx) % wide
            piece = pltpu.roll(piece, shift, 1) if shift else piece
            packed = jnp.where(slot == m, piece, packed)
        s1[:, xx : xx + 1, :] = packed.reshape(xy, 1, wide)

    def everyone(axis, size, mine, src_of, dst, send, recv):
        def copy_to(i):
            to = lax.rem(mine + i, size)
            return remote(src_of(to), dst.at[mine], send.at[to], recv.at[mine], {axis: to})

        def copy_from(i):
            to = lax.rem(mine + i, size)
            return remote(src_of(to), dst.at[to], send.at[to], recv.at[to], {axis: to})

        def go(i, carry):
            copy_to(i).start()
            return carry

        def done(i, carry):
            copy_from(i).wait()
            return carry

        lax.fori_loop(1, size, go, 0)
        dst[mine] = src_of(mine)[...]
        lax.fori_loop(1, size, done, 0)

    everyone("xy", xy, me, lambda to: s1.at[to], r1, a1s, a1r)
    gathered = jnp.concatenate([r1[:, 0:1, :].reshape(xy, wide), r1[:, 1:2, :].reshape(xy, wide)], axis=0)
    fz[...] = lax.dot_general(
        gathered, fx[...], (((0,), (0,)), ((), ())),
        precision=HIGH, preferred_element_type=jnp.float32,
    ).reshape(coarse, M, 2 * half)

    up = lax.broadcasted_iota(jnp.int32, (M, 2 * half), 1) < half
    theta = th[...]
    decay = jnp.exp(-theta)
    state = jnp.zeros((M, 2 * half), jnp.float32)
    for t in range(coarse):
        state = decay * state + jnp.where(up, fz[t], fz[coarse - 1 - t])
        wz[t] = state
    ztile[...] = state
    everyone("gz", gz, q, lambda to: ztile, zr, gs, gr)
    block = jnp.exp(-float(coarse) * theta)
    total = jnp.zeros((M, 2 * half), jnp.float32)
    inflow = jnp.zeros((M, 2 * half), jnp.float32)
    steps_in = jnp.where(up, q, gz - 1 - q)
    for t in range(gz):
        inflow = jnp.where(steps_in == t, total, inflow)
        total = block * total + jnp.where(up, zr[t], zr[gz - 1 - t])
    span = float(coarse * gz + 1)
    image = pltpu.roll(total, half, 1) - jnp.exp(-span * theta) * total
    image = image * jnp.exp(-theta * (float(coarse) * steps_in.astype(jnp.float32) + 1.0))
    inflow = inflow - image / (1.0 - jnp.exp(-2.0 * span * theta))
    scale = 1.0 / (jnp.exp(theta) - decay)
    power = decay
    for t in range(coarse):
        wz[t] = wz[t] + power * inflow
        power = power * decay
    last = decay * wz[coarse - 1]
    beyond = scale * (last + pltpu.roll(inflow, half, 1))
    above, below = beyond * high, beyond * low
    above = pltpu.roll(above, half, 1)
    for z in range(coarse):
        value = scale * (wz[z] + pltpu.roll(wz[coarse - 1 - z], half, 1) - fz[z])
        ring = below if z == 0 else above if z == 1 else 0.0
        vz[z] = jnp.where(up, value, ring)
    s2[...] = lax.dot_general(
        bx[...], vz[...].reshape(wide, 2 * half), (((1,), (1,)), ((), ())),
        precision=HIGH, preferred_element_type=jnp.float32,
    ).reshape(xy, 8, wide)
    everyone("xy", xy, me, lambda to: s2.at[to], r2, a2s, a2r)

    def spread(base):
        parts = [r2[:, base + e : base + e + 1, :].reshape(xy, wide) for e in range(4)]
        modes = []
        for m in range(M):
            mixed = jnp.zeros((xy, wide), jnp.float32)
            for e in range(4):
                shift = (2 * e - m) % wide
                piece = pltpu.roll(parts[e], shift, 1) if shift else parts[e]
                mixed = jnp.where(slot == 2 * e, piece, mixed)
            modes.append(mixed + pltpu.roll(mixed, 1, 1))
        return jnp.concatenate(modes, axis=0)

    turned = jnp.concatenate([spread(0).T, spread(4).T[:16]], axis=0)
    cc[...] = jnp.dot(
        turned, ty[...], precision=HIGH, preferred_element_type=jnp.float32
    ).reshape(coarse + 2, 8, ny)

    def lift(z, carry):
        fix = cc[z]
        pa[2 * z + 2] = pa[2 * z + 2] + fix
        pa[2 * z + 3] = pa[2 * z + 3] + fix
        return carry

    lax.fori_loop(0, coarse, lift, 0)
    for i, z in ((0, coarse), (1, coarse), (planes + 2, coarse + 1), (planes + 3, coarse + 1)):
        pa[i] = pa[i] + cc[z]
    wide_sweep()

    def last_sweep(i, carry):
        out_ref[i - 2] = relax(pb, i)[2:6, :]
        return carry

    lax.fori_loop(2, planes + 2, last_sweep, 0, unroll=2)


def body(gz, xy, consts, source, potential):
    planes, rows, ny = source.shape
    coarse = planes // 2
    wide, two = coarse * 8, 4 * xy
    f32 = jnp.float32
    vm = lambda *shape: pltpu.VMEM(shape, f32)
    dma = lambda n: pltpu.SemaphoreType.DMA((n,))
    scratch = [
        vm(planes, rows, ny), vm(planes, rows, ny), vm(M * xy, ny), vm(2 * xy, two), vm(8 * xy, two), vm(M, two),
        vm(planes + 4, 8, ny), vm(planes + 4, 8, ny), vm(planes + 2, 8, ny),
        vm(2, planes, 2, ny), vm(2, planes, 2, ny), vm(2, planes, 1, ny), vm(2, planes, 1, ny),
        vm(2, 2, rows, ny), vm(2, 1, rows, ny), vm(4, 1, ny), vm(4, 1, ny),
        vm(2, planes, 2, ny), vm(2, planes, 2, ny), vm(2, 2, 8, ny), vm(4, 1, ny), vm(4, 1, ny),
        vm(coarse, 8, ny), vm(xy, 2, wide), vm(xy, 2, wide), vm(coarse, M, two), vm(coarse, M, two),
        vm(M, two), vm(gz, M, two), vm(coarse, M, two), vm(xy, 8, wide), vm(xy, 8, wide), vm(coarse + 2, 8, ny),
        dma(6), dma(12), dma(12), dma(8), dma(8), dma(xy), dma(xy), dma(gz), dma(gz), dma(xy), dma(xy),
    ]
    hbm = pl.BlockSpec(memory_space=pl.ANY)
    return pl.pallas_call(
        functools.partial(kernel, gz, xy),
        out_shape=jax.ShapeDtypeStruct(source.shape, f32),
        in_specs=[hbm] * 6,
        out_specs=pl.BlockSpec(memory_space=pltpu.VMEM),
        scratch_shapes=scratch,
        compiler_params=pltpu.CompilerParams(collective_id=0, has_side_effects=True),
        name="vcycle",
    )(source, potential, *[jnp.asarray(c) for c in consts])


def solution(mesh):
    gz, xy = mesh.shape["gz"], mesh.shape["xy"]
    consts = tables(xy)
    placed = (P("gz", "xy", None), P("gz", "xy", None))
    return jax.shard_map(
        functools.partial(body, gz, xy, consts), mesh=mesh, in_specs=placed,
        out_specs=P("gz", "xy", None), check_vma=False,
    )
```

```python
import functools
import math

import jax
import jax.numpy as jnp
import numpy as np
from jax import lax
from jax.experimental import pallas as pl
from jax.experimental.pallas import tpu as pltpu
from jax.sharding import PartitionSpec as P

SCREEN = 64
OMEGA = 0.8
KAPPA = 1.0 / (SCREEN * SCREEN)
CW = 6.0 + KAPPA
HIGH = lax.Precision.HIGHEST
M = 8
CORNERS = ((-1, -1), (-1, 1), (1, -1), (1, 1))


def sine(count):
    idx = np.arange(1, count + 1, dtype=np.int64)
    turns = idx[:, None] * idx[None, :] % (2 * (count + 1))
    return math.sqrt(2.0 / (count + 1)) * np.sin(math.pi / (count + 1) * turns)


def eigen(count):
    return 2.0 - 2.0 * np.cos(math.pi / (count + 1) * np.arange(1, count + 1))


def tables(groups):
    nx, ny = 2 * groups, M * groups
    sx, sy = sine(nx), sine(ny)
    ty = np.repeat(sy, 2, axis=1)
    order = np.concatenate([np.arange(0, nx, 2), np.arange(1, nx, 2)])
    fx = 0.5 * np.concatenate([sx[order], sx[order]], axis=1)
    bx = np.zeros((groups, 8, 2 * nx))
    for d in range(groups):
        for e in range(4):
            x = 2 * d - 1 + e
            if 0 <= x < nx:
                bx[d, e, :nx] = sx[x]
                bx[d, 4 + e, nx:] = sx[x]
    diag = 2.0 + eigen(nx)[None, None, :] + eigen(ny).reshape(M, groups).T[:, :, None] + 4.0 * KAPPA
    theta = np.arccosh(0.5 * diag)
    theta = np.concatenate([theta, theta], axis=2)
    f = lambda t: np.asarray(t, np.float32)
    return f(ty), f(fx), f(bx.reshape(groups * 8, 2 * nx)), f(theta)


def kernel(
    gz, xy, src_hbm, pot_hbm, ty_hbm, fx_hbm, bx_hbm, th_hbm, out_ref,
    potv, srcv, ty, fx, bx, th, pa, pb, sv,
    xps, xpr, xts, xtr, xss, xsr, zpr, zsr, cs, cr,
    xqs, xqr, zqr, ds, dr,
    rs, s1, r1, fz, wz, ztile, zr, vz, s2, r2, cc,
    ld, e1s, e1r, e2s, e2r, a1s, a1r, gs, gr, a2s, a2r, known_x, known_z,
):
    q, me = lax.axis_index("gz"), lax.axis_index("xy")
    planes, rows, ny = potv.shape
    half = 2 * xy
    top = planes + 3

    loads = [
        pltpu.make_async_copy(pot_hbm, potv, ld.at[0]),
        pltpu.make_async_copy(src_hbm, srcv, ld.at[1]),
        pltpu.make_async_copy(ty_hbm, ty, ld.at[2]),
        pltpu.make_async_copy(fx_hbm, fx, ld.at[3]),
        pltpu.make_async_copy(bx_hbm, bx, ld.at[4]),
        pltpu.make_async_copy(th_hbm.at[me], th, ld.at[5]),
    ]
    for copy in loads:
        copy.start()

    def shifted(dz, dx):
        where = {}
        if dz:
            where["gz"] = lax.rem(q + dz + gz, gz)
        if dx:
            where["xy"] = lax.rem(me + dx + xy, xy)
        return where

    def tell(sem, where):
        pl.semaphore_signal(sem, inc=1, device_id=where, device_id_type=pl.DeviceIdType.MESH)

    barrier = pltpu.get_barrier_semaphore()
    for dz, dx in CORNERS + ((-1, 0), (1, 0), (0, -1), (0, 1)):
        tell(barrier, shifted(dz, dx))

    pa[...] = jnp.zeros_like(pa)
    sv[...] = jnp.zeros_like(sv)
    for side in range(2):
        xtr[side, 0:2] = jnp.zeros((2, 1, ny), jnp.float32)
        xtr[side, planes + 2 : planes + 4] = jnp.zeros((2, 1, ny), jnp.float32)
    loads[0].wait()
    loads[1].wait()
    xps[0] = potv[:, 0:2, :]
    xps[1] = potv[:, 2:4, :]
    xts[0] = potv[:, 2:3, :]
    xts[1] = potv[:, 1:2, :]
    xss[0] = srcv[:, 0:2, :]
    xss[1] = srcv[:, 2:4, :]
    for c, (dz, dx) in enumerate(CORNERS):
        z0, z1 = (0, 1) if dz < 0 else (planes - 1, planes - 2)
        x0, x1 = (0, 1) if dx < 0 else (rows - 1, rows - 2)
        cs[c, 0:1] = potv[z0, x0 : x0 + 1, :]
        cs[c, 1:2] = potv[z0, x1 : x1 + 1, :]
        cs[c, 2:3] = potv[z1, x0 : x0 + 1, :]
        cs[c, 3:4] = srcv[z0, x0 : x0 + 1, :]
    pl.semaphore_wait(barrier, 8)

    def round_of(level):
        for axis, size, dim, known in (("xy", xy, 1, known_x), ("gz", gz, 0, known_z)):
            reach = 2**level
            if level and reach // 2 < size // 2:
                pl.semaphore_wait(known.at[level - 1], 2)
            if reach < size // 2:
                for way in (-reach, reach):
                    tell(known.at[level], shifted(way, 0) if dim == 0 else shifted(0, way))

    round_of(0)

    class Exchange:
        def __init__(self, send, recv):
            self.send, self.recv, self.copies = send, recv, []

        def add(self, src, dst, dz, dx):
            slot = len(self.copies)
            copy = remote(src, dst, self.send.at[slot], self.recv.at[slot], shifted(dz, dx))
            self.copies.append((copy, exists(dz, dx), exists(-dz, -dx)))

        def start(self):
            for copy, there, unused in self.copies:
                pl.when(there)(copy.start)

        def wait(self):
            for copy, there, back in self.copies:
                pl.when(back)(copy.wait_recv)
                pl.when(there)(copy.wait_send)

    def exists(dz, dx):
        there = None
        for step, mine, size in ((dz, q, gz), (dx, me, xy)):
            if step:
                ok = mine > 0 if step < 0 else mine < size - 1
                there = ok if there is None else jnp.logical_and(there, ok)
        return there

    def remote(src, dst, send, recv, where):
        return pltpu.make_async_remote_copy(
            src_ref=src, dst_ref=dst, send_sem=send, recv_sem=recv,
            device_id=where, device_id_type=pl.DeviceIdType.MESH,
        )

    first = Exchange(e1s, e1r)
    for side, step in ((0, -1), (1, 1)):
        first.add(xps.at[side], xpr.at[side], 0, step)
        first.add(xts.at[side], xtr.at[side, pl.ds(2, planes)], 0, step)
        first.add(xss.at[side], xsr.at[side], 0, step)
        first.add(potv.at[pl.ds(0 if step < 0 else planes - 3, 3)], zpr.at[side], step, 0)
        first.add(srcv.at[pl.ds(0 if step < 0 else planes - 2, 2)], zsr.at[side], step, 0)
    for c, (dz, dx) in enumerate(CORNERS):
        first.add(cs.at[c], cr.at[c], dz, dx)
    first.start()

    pa[3:top, 2:6, :] = potv[...]
    sv[2 : planes + 2, 2:6, :] = srcv[...]
    sub = lax.broadcasted_iota(jnp.int32, (8, ny), 0)
    lane = lax.broadcasted_iota(jnp.int32, (8, ny), 1)
    inside = jnp.logical_and(
        jnp.logical_or(sub >= 2, me > 0), jnp.logical_or(sub < 6, me < xy - 1)
    )
    has_low, has_high, has_near, has_far = q > 0, q < gz - 1, me > 0, me < xy - 1

    def corner_places(dz, dx):
        z0, z1 = (top, top + 1) if dz < 0 else (2, 1)
        x0, x1 = (6, 7) if dx < 0 else (1, 0)
        return z0, z1, x0, x1, exists(-dz, -dx)

    first.wait()
    round_of(1)
    pa[3:top, 0:2, :] = jnp.where(has_near, xpr[1], 0.0)
    pa[3:top, 6:8, :] = jnp.where(has_far, xpr[0], 0.0)
    pa[0:3, 2:6, :] = jnp.where(has_low, zpr[1], 0.0)
    pa[top : top + 3, 2:6, :] = jnp.where(has_high, zpr[0], 0.0)
    sv[2 : planes + 2, 0:2, :] = jnp.where(has_near, xsr[1], 0.0)
    sv[2 : planes + 2, 6:8, :] = jnp.where(has_far, xsr[0], 0.0)
    sv[0:2, 2:6, :] = jnp.where(has_low, zsr[1], 0.0)
    sv[planes + 2 : planes + 4, 2:6, :] = jnp.where(has_high, zsr[0], 0.0)
    for c, (dz, dx) in enumerate(CORNERS):
        z0, z1, x0, x1, there = corner_places(dz, dx)
        corner = jnp.where(there, cr[c], 0.0)
        pa[z0, x0 : x0 + 1, :] = corner[0:1]
        pa[z0, x1 : x1 + 1, :] = corner[1:2]
        pa[z1, x0 : x0 + 1, :] = corner[2:3]
        sv[z0 - 1, x0 : x0 + 1, :] = corner[3:4]

    def neighbours(ref, i, ends=None):
        v = ref[i]
        total = ref[i - 1] + ref[i + 1]
        back, forth = pltpu.roll(v, 1, 0), pltpu.roll(v, 7, 0)
        if ends is not None:
            back, forth = jnp.where(sub == 0, ends[0], back), jnp.where(sub == 7, ends[1], forth)
        total = total + back + forth
        total = total + jnp.where(lane == 0, 0.0, pltpu.roll(v, 1, 1))
        total = total + jnp.where(lane == ny - 1, 0.0, pltpu.roll(v, ny - 1, 1))
        return v, total

    def relax(ref, i, ends=None):
        v, total = neighbours(ref, i, ends)
        return (1.0 - OMEGA) * v + (OMEGA / CW) * (sv[i - 1] + total)

    def sweep(src, dst, ring, ended=False):
        def step(i, carry):
            ends = None
            if ended:
                ends = [jnp.where(there, xtr[side, i - 1], 0.0) for there, side in ((has_near, 1), (has_far, 0))]
            dst[i] = jnp.where(inside, relax(src, i, ends), 0.0)
            return carry

        lax.fori_loop(3 - ring, top + ring, step, 0, unroll=2)
        for i in range(ring):
            dst[2 - i] = jnp.where(has_low, dst[2 - i], 0.0)
            dst[top + i] = jnp.where(has_high, dst[top + i], 0.0)

    sweep(pa, pb, 2, True)
    round_of(2)
    sweep(pb, pa, 1)

    xqs[0] = pa[3:top, 2:4, :]
    xqs[1] = pa[3:top, 4:6, :]
    for c, (dz, dx) in enumerate(CORNERS):
        z, x = 3 if dz < 0 else top - 1, 2 if dx < 0 else 5
        ds[c] = pa[z, x : x + 1, :]
    second = Exchange(e2s, e2r)
    for side, step in ((0, -1), (1, 1)):
        second.add(xqs.at[side], xqr.at[side], 0, step)
        second.add(pa.at[pl.ds(3 if step < 0 else top - 2, 2)], zqr.at[side], step, 0)
    for c, (dz, dx) in enumerate(CORNERS):
        second.add(ds.at[c], dr.at[c], dz, dx)
    second.start()
    round_of(3)

    def residual(i):
        v, total = neighbours(pa, i)
        return sv[i - 1] - CW * v + total

    def coarsen(z, carry):
        rs[z] = residual(2 * z + 3) + residual(2 * z + 4)
        return carry

    coarse = planes // 2
    lax.fori_loop(0, coarse, coarsen, 0)
    for copy in loads[2:]:
        copy.wait()
    wide = coarse * 8
    spec = lax.dot_general(
        ty[...], rs[...].reshape(wide, ny), (((1,), (1,)), ((), ())),
        precision=HIGH, preferred_element_type=jnp.float32,
    )
    spec = spec + pltpu.roll(spec, wide - 1, 1)
    slot = lax.broadcasted_iota(jnp.int32, (xy, wide), 1) % 8
    for xx in range(2):
        packed = jnp.zeros((xy, wide), jnp.float32)
        for m in range(M):
            piece = spec[m * xy : (m + 1) * xy, :]
            shift = (m - 2 - 2 * xx) % wide
            piece = pltpu.roll(piece, shift, 1) if shift else piece
            packed = jnp.where(slot == m, piece, packed)
        s1[:, xx : xx + 1, :] = packed.reshape(xy, 1, wide)

    def everyone(axis, size, mine, src_of, dst, send, recv):
        def copy_to(i):
            to = lax.rem(mine + i, size)
            return remote(src_of(to), dst.at[mine], send.at[to], recv.at[mine], {axis: to})

        def copy_from(i):
            to = lax.rem(mine + i, size)
            return remote(src_of(to), dst.at[to], send.at[to], recv.at[to], {axis: to})

        def go(i, carry):
            copy_to(i).start()
            return carry

        def done(i, carry):
            copy_from(i).wait()
            return carry

        lax.fori_loop(1, size, go, 0)
        dst[mine] = src_of(mine)[...]
        lax.fori_loop(1, size, done, 0)

    round_of(4)
    everyone("xy", xy, me, lambda to: s1.at[to], r1, a1s, a1r)
    gathered = jnp.concatenate([r1[:, 0:1, :].reshape(xy, wide), r1[:, 1:2, :].reshape(xy, wide)], axis=0)
    fz[...] = lax.dot_general(
        gathered, fx[...], (((0,), (0,)), ((), ())),
        precision=HIGH, preferred_element_type=jnp.float32,
    ).reshape(coarse, M, 2 * half)

    up = lax.broadcasted_iota(jnp.int32, (M, 2 * half), 1) < half
    theta = th[...]
    decay = jnp.exp(-theta)
    state = jnp.zeros((M, 2 * half), jnp.float32)
    for t in range(coarse):
        state = decay * state + jnp.where(up, fz[t], fz[coarse - 1 - t])
        wz[t] = state
    ztile[...] = state
    everyone("gz", gz, q, lambda to: ztile, zr, gs, gr)
    block = jnp.exp(-float(coarse) * theta)
    total = jnp.zeros((M, 2 * half), jnp.float32)
    inflow = jnp.zeros((M, 2 * half), jnp.float32)
    steps_in = jnp.where(up, q, gz - 1 - q)
    for t in range(gz):
        inflow = jnp.where(steps_in == t, total, inflow)
        total = block * total + jnp.where(up, zr[t], zr[gz - 1 - t])
    span = float(coarse * gz + 1)
    image = pltpu.roll(total, half, 1) - jnp.exp(-span * theta) * total
    image = image * jnp.exp(-theta * (float(coarse) * steps_in.astype(jnp.float32) + 1.0))
    inflow = inflow - image / (1.0 - jnp.exp(-2.0 * span * theta))
    scale = 1.0 / (jnp.exp(theta) - decay)
    power = decay
    for t in range(coarse):
        wz[t] = wz[t] + power * inflow
        power = power * decay
    last = decay * wz[coarse - 1]
    beyond = scale * (last + pltpu.roll(inflow, half, 1))
    above, below = jnp.where(has_high, beyond, 0.0), jnp.where(has_low, beyond, 0.0)
    above = pltpu.roll(above, half, 1)
    for z in range(coarse):
        value = scale * (wz[z] + pltpu.roll(wz[coarse - 1 - z], half, 1) - fz[z])
        ring = below if z == 0 else above if z == 1 else 0.0
        vz[z] = jnp.where(up, value, ring)
    s2[...] = lax.dot_general(
        bx[...], vz[...].reshape(wide, 2 * half), (((1,), (1,)), ((), ())),
        precision=HIGH, preferred_element_type=jnp.float32,
    ).reshape(xy, 8, wide)
    everyone("xy", xy, me, lambda to: s2.at[to], r2, a2s, a2r)

    def spread(base):
        parts = [r2[:, base + e : base + e + 1, :].reshape(xy, wide) for e in range(4)]
        modes = []
        for m in range(M):
            mixed = jnp.zeros((xy, wide), jnp.float32)
            for e in range(4):
                shift = (2 * e - m) % wide
                piece = pltpu.roll(parts[e], shift, 1) if shift else parts[e]
                mixed = jnp.where(slot == 2 * e, piece, mixed)
            modes.append(mixed + pltpu.roll(mixed, 1, 1))
        return jnp.concatenate(modes, axis=0)

    turned = jnp.concatenate([spread(0).T, spread(4).T[:16]], axis=0)
    cc[...] = jnp.dot(
        turned, ty[...], precision=HIGH, preferred_element_type=jnp.float32
    ).reshape(coarse + 2, 8, ny)

    second.wait()
    pa[3:top, 0:2, :] = jnp.where(has_near, xqr[1], 0.0)
    pa[3:top, 6:8, :] = jnp.where(has_far, xqr[0], 0.0)
    pa[1:3, 2:6, :] = jnp.where(has_low, zqr[1, :, 2:6, :], 0.0)
    pa[top : top + 2, 2:6, :] = jnp.where(has_high, zqr[0, :, 2:6, :], 0.0)
    for c, (dz, dx) in enumerate(CORNERS):
        z0, z1, x0, x1, there = corner_places(dz, dx)
        pa[z0, x0 : x0 + 1, :] = jnp.where(there, dr[c], 0.0)

    def lift(z, carry):
        fix = cc[z]
        pa[2 * z + 3] = pa[2 * z + 3] + fix
        pa[2 * z + 4] = pa[2 * z + 4] + fix
        return carry

    lax.fori_loop(0, coarse, lift, 0)
    for i, z in ((1, coarse), (2, coarse), (top, coarse + 1), (top + 1, coarse + 1)):
        pa[i] = pa[i] + cc[z]
    sweep(pa, pb, 1)

    def last_sweep(i, carry):
        out_ref[i - 3] = relax(pb, i)[2:6, :]
        return carry

    lax.fori_loop(3, top, last_sweep, 0, unroll=2)


def body(gz, xy, consts, source, potential):
    planes, rows, ny = source.shape
    coarse = planes // 2
    wide, two = coarse * 8, 4 * xy
    f32 = jnp.float32
    vm = lambda *shape: pltpu.VMEM(shape, f32)
    dma = lambda n: pltpu.SemaphoreType.DMA((n,))
    scratch = [
        vm(planes, rows, ny), vm(planes, rows, ny), vm(M * xy, ny), vm(2 * xy, two), vm(8 * xy, two), vm(M, two),
        vm(planes + 6, 8, ny), vm(planes + 6, 8, ny), vm(planes + 4, 8, ny),
        vm(2, planes, 2, ny), vm(2, planes, 2, ny), vm(2, planes, 1, ny), vm(2, planes + 4, 1, ny),
        vm(2, planes, 2, ny), vm(2, planes, 2, ny),
        vm(2, 3, rows, ny), vm(2, 2, rows, ny), vm(4, 4, ny), vm(4, 4, ny),
        vm(2, planes, 2, ny), vm(2, planes, 2, ny), vm(2, 2, 8, ny), vm(4, 1, ny), vm(4, 1, ny),
        vm(coarse, 8, ny), vm(xy, 2, wide), vm(xy, 2, wide), vm(coarse, M, two), vm(coarse, M, two),
        vm(M, two), vm(gz, M, two), vm(coarse, M, two), vm(xy, 8, wide), vm(xy, 8, wide), vm(coarse + 2, 8, ny),
        dma(6), dma(14), dma(14), dma(8), dma(8), dma(xy), dma(xy), dma(gz), dma(gz), dma(xy), dma(xy),
        pltpu.SemaphoreType.REGULAR((4,)), pltpu.SemaphoreType.REGULAR((4,)),
    ]
    hbm = pl.BlockSpec(memory_space=pl.ANY)
    return pl.pallas_call(
        functools.partial(kernel, gz, xy),
        out_shape=jax.ShapeDtypeStruct(source.shape, f32),
        in_specs=[hbm] * 6,
        out_specs=pl.BlockSpec(memory_space=pltpu.VMEM),
        scratch_shapes=scratch,
        compiler_params=pltpu.CompilerParams(collective_id=0, has_side_effects=True),
        name="vcycle",
    )(source, potential, *[jnp.asarray(c) for c in consts])


def solution(mesh):
    gz, xy = mesh.shape["gz"], mesh.shape["xy"]
    consts = tables(xy)
    placed = (P("gz", "xy", None), P("gz", "xy", None))
    return jax.shard_map(
        functools.partial(body, gz, xy, consts), mesh=mesh, in_specs=placed,
        out_specs=P("gz", "xy", None), check_vma=False,
    )
```

```python
import functools
import math

import jax
import jax.numpy as jnp
import ml_dtypes
import numpy as np
from jax import lax
from jax.experimental import pallas as pl
from jax.experimental.pallas import tpu as pltpu
from jax.sharding import PartitionSpec as P

SCREEN = 64
OMEGA = 0.8
KAPPA = 1.0 / (SCREEN * SCREEN)
CW = 6.0 + KAPPA
M = 8
CORNERS = ((-1, -1), (-1, 1), (1, -1), (1, 1))


def sine(count):
    idx = np.arange(1, count + 1, dtype=np.int64)
    turns = idx[:, None] * idx[None, :] % (2 * (count + 1))
    return math.sqrt(2.0 / (count + 1)) * np.sin(math.pi / (count + 1) * turns)


def eigen(count):
    return 2.0 - 2.0 * np.cos(math.pi / (count + 1) * np.arange(1, count + 1))


def two_parts(table):
    coarse = table.astype(ml_dtypes.bfloat16)
    return np.stack([coarse, (table - coarse.astype(np.float64)).astype(ml_dtypes.bfloat16)])


def dot3(value, table, dims):
    coarse = value.astype(jnp.bfloat16)
    fine = (value - coarse.astype(jnp.float32)).astype(jnp.bfloat16)
    dot = lambda a, b: lax.dot_general(a, b, (dims, ((), ())), preferred_element_type=jnp.float32)
    return dot(coarse, table[0]) + dot(fine, table[0]) + dot(coarse, table[1])


def dot3_table_first(table, value, dims):
    coarse = value.astype(jnp.bfloat16)
    fine = (value - coarse.astype(jnp.float32)).astype(jnp.bfloat16)
    dot = lambda a, b: lax.dot_general(a, b, (dims, ((), ())), preferred_element_type=jnp.float32)
    return dot(table[0], coarse) + dot(table[0], fine) + dot(table[1], coarse)


def tables(groups):
    nx, ny = 2 * groups, M * groups
    sx, sy = sine(nx), sine(ny)
    ty = np.repeat(sy, 2, axis=1)
    order = np.concatenate([np.arange(0, nx, 2), np.arange(1, nx, 2)])
    fx = 0.5 * np.concatenate([sx[order], sx[order]], axis=1)
    bx = np.zeros((groups, 8, 2 * nx))
    for d in range(groups):
        for e in range(4):
            x = 2 * d - 1 + e
            if 0 <= x < nx:
                bx[d, e, :nx] = sx[x]
                bx[d, 4 + e, nx:] = sx[x]
    diag = 2.0 + eigen(nx)[None, None, :] + eigen(ny).reshape(M, groups).T[:, :, None] + 4.0 * KAPPA
    theta = np.arccosh(0.5 * diag)
    theta = np.concatenate([theta, theta], axis=2)
    return two_parts(ty), two_parts(fx), two_parts(bx.reshape(groups * 8, 2 * nx)), theta.astype(np.float32)


def kernel(
    gz, xy, src_hbm, pot_hbm, ty_hbm, fx_hbm, bx_hbm, th_hbm, out_ref,
    potv, srcv, ty, fx, bx, th, pa, pb, sv,
    xps, xpr, xts, xtr, xss, xsr, zpr, zsr, cs, cr,
    xqs, xqr, zqr, ds, dr,
    rs, s1, r1, fz, wz, ztile, zr, vz, s2, r2, tm, cc,
    ld, e1s, e1r, e2s, e2r, a1s, a1r, gs, gr, a2s, a2r, known_x, known_z,
):
    q, me = lax.axis_index("gz"), lax.axis_index("xy")
    planes, rows, ny = potv.shape
    half = 2 * xy
    top = planes + 3

    loads = [
        pltpu.make_async_copy(pot_hbm, potv, ld.at[0]),
        pltpu.make_async_copy(src_hbm, srcv, ld.at[1]),
        pltpu.make_async_copy(ty_hbm, ty, ld.at[2]),
        pltpu.make_async_copy(fx_hbm, fx, ld.at[3]),
        pltpu.make_async_copy(bx_hbm, bx, ld.at[4]),
        pltpu.make_async_copy(th_hbm.at[me], th, ld.at[5]),
    ]
    def shifted(dz, dx):
        where = {}
        if dz:
            where["gz"] = lax.rem(q + dz + gz, gz)
        if dx:
            where["xy"] = lax.rem(me + dx + xy, xy)
        return where

    def tell(sem, where):
        pl.semaphore_signal(sem, inc=1, device_id=where, device_id_type=pl.DeviceIdType.MESH)

    barrier = pltpu.get_barrier_semaphore()
    for dz, dx in CORNERS + ((-1, 0), (1, 0), (0, -1), (0, 1)):
        tell(barrier, shifted(dz, dx))
    loads[0].start()
    loads[1].start()

    pa[...] = jnp.zeros_like(pa)
    sv[...] = jnp.zeros_like(sv)
    for side in range(2):
        xtr[side, 0:2] = jnp.zeros((2, 1, ny), jnp.float32)
        xtr[side, planes + 2 : planes + 4] = jnp.zeros((2, 1, ny), jnp.float32)
    loads[0].wait()
    loads[1].wait()
    xps[0] = potv[:, 0:2, :]
    xps[1] = potv[:, 2:4, :]
    xts[0] = potv[:, 2:3, :]
    xts[1] = potv[:, 1:2, :]
    xss[0] = srcv[:, 0:2, :]
    xss[1] = srcv[:, 2:4, :]
    for c, (dz, dx) in enumerate(CORNERS):
        z0, z1 = (0, 1) if dz < 0 else (planes - 1, planes - 2)
        x0, x1 = (0, 1) if dx < 0 else (rows - 1, rows - 2)
        cs[c, 0:1] = potv[z0, x0 : x0 + 1, :]
        cs[c, 1:2] = potv[z0, x1 : x1 + 1, :]
        cs[c, 2:3] = potv[z1, x0 : x0 + 1, :]
        cs[c, 3:4] = srcv[z0, x0 : x0 + 1, :]
    pl.semaphore_wait(barrier, 8)

    def round_of(level):
        for axis, size, dim, known in (("xy", xy, 1, known_x), ("gz", gz, 0, known_z)):
            reach = 2**level
            if level and reach // 2 < size // 2:
                pl.semaphore_wait(known.at[level - 1], 2)
            if reach < size // 2:
                for way in (-reach, reach):
                    tell(known.at[level], shifted(way, 0) if dim == 0 else shifted(0, way))

    round_of(0)

    class Exchange:
        def __init__(self, send, recv):
            self.send, self.recv, self.copies = send, recv, []

        def add(self, src, dst, dz, dx):
            slot = len(self.copies)
            copy = remote(src, dst, self.send.at[slot], self.recv.at[slot], shifted(dz, dx))
            self.copies.append((copy, exists(dz, dx), exists(-dz, -dx)))

        def start(self):
            for copy, there, unused in self.copies:
                pl.when(there)(copy.start)

        def wait(self):
            for copy, there, back in self.copies:
                pl.when(back)(copy.wait_recv)
                pl.when(there)(copy.wait_send)

    def exists(dz, dx):
        there = None
        for step, mine, size in ((dz, q, gz), (dx, me, xy)):
            if step:
                ok = mine > 0 if step < 0 else mine < size - 1
                there = ok if there is None else jnp.logical_and(there, ok)
        return there

    def remote(src, dst, send, recv, where):
        return pltpu.make_async_remote_copy(
            src_ref=src, dst_ref=dst, send_sem=send, recv_sem=recv,
            device_id=where, device_id_type=pl.DeviceIdType.MESH,
        )

    first = Exchange(e1s, e1r)
    for side, step in ((0, -1), (1, 1)):
        first.add(xps.at[side], xpr.at[side], 0, step)
        first.add(xts.at[side], xtr.at[side, pl.ds(2, planes)], 0, step)
        first.add(xss.at[side], xsr.at[side], 0, step)
        first.add(potv.at[pl.ds(0 if step < 0 else planes - 3, 3)], zpr.at[side], step, 0)
        first.add(srcv.at[pl.ds(0 if step < 0 else planes - 2, 2)], zsr.at[side], step, 0)
    for c, (dz, dx) in enumerate(CORNERS):
        first.add(cs.at[c], cr.at[c], dz, dx)
    first.start()
    for copy in loads[2:]:
        copy.start()

    pa[3:top, 2:6, :] = potv[...]
    sv[2 : planes + 2, 2:6, :] = srcv[...]
    sub = lax.broadcasted_iota(jnp.int32, (8, ny), 0)
    lane = lax.broadcasted_iota(jnp.int32, (8, ny), 1)
    inside = jnp.logical_and(
        jnp.logical_or(sub >= 2, me > 0), jnp.logical_or(sub < 6, me < xy - 1)
    )
    has_low, has_high, has_near, has_far = q > 0, q < gz - 1, me > 0, me < xy - 1

    def corner_places(dz, dx):
        z0, z1 = (top, top + 1) if dz < 0 else (2, 1)
        x0, x1 = (6, 7) if dx < 0 else (1, 0)
        return z0, z1, x0, x1, exists(-dz, -dx)

    first.wait()
    round_of(1)
    pa[3:top, 0:2, :] = jnp.where(has_near, xpr[1], 0.0)
    pa[3:top, 6:8, :] = jnp.where(has_far, xpr[0], 0.0)
    pa[0:3, 2:6, :] = jnp.where(has_low, zpr[1], 0.0)
    pa[top : top + 3, 2:6, :] = jnp.where(has_high, zpr[0], 0.0)
    sv[2 : planes + 2, 0:2, :] = jnp.where(has_near, xsr[1], 0.0)
    sv[2 : planes + 2, 6:8, :] = jnp.where(has_far, xsr[0], 0.0)
    sv[0:2, 2:6, :] = jnp.where(has_low, zsr[1], 0.0)
    sv[planes + 2 : planes + 4, 2:6, :] = jnp.where(has_high, zsr[0], 0.0)
    for c, (dz, dx) in enumerate(CORNERS):
        z0, z1, x0, x1, there = corner_places(dz, dx)
        corner = jnp.where(there, cr[c], 0.0)
        pa[z0, x0 : x0 + 1, :] = corner[0:1]
        pa[z0, x1 : x1 + 1, :] = corner[1:2]
        pa[z1, x0 : x0 + 1, :] = corner[2:3]
        sv[z0 - 1, x0 : x0 + 1, :] = corner[3:4]

    def neighbours(ref, i, ends=None):
        v = ref[i]
        total = ref[i - 1] + ref[i + 1]
        back, forth = pltpu.roll(v, 1, 0), pltpu.roll(v, 7, 0)
        if ends is not None:
            back, forth = jnp.where(sub == 0, ends[0], back), jnp.where(sub == 7, ends[1], forth)
        total = total + back + forth
        total = total + jnp.where(lane == 0, 0.0, pltpu.roll(v, 1, 1))
        total = total + jnp.where(lane == ny - 1, 0.0, pltpu.roll(v, ny - 1, 1))
        return v, total

    def relax(ref, i, ends=None):
        v, total = neighbours(ref, i, ends)
        return (1.0 - OMEGA) * v + (OMEGA / CW) * (sv[i - 1] + total)

    def sweep(src, dst, ring, ended=False):
        def step(i, carry):
            ends = None
            if ended:
                ends = [jnp.where(there, xtr[side, i - 1], 0.0) for there, side in ((has_near, 1), (has_far, 0))]
            dst[i] = jnp.where(inside, relax(src, i, ends), 0.0)
            return carry

        if ring == 2:
            lax.fori_loop(1, top + 2, step, 0, unroll=4)
        else:
            lax.fori_loop(3, top, step, 0, unroll=4)
            step(2, 0)
            step(top, 0)
        for i in range(ring):
            dst[2 - i] = jnp.where(has_low, dst[2 - i], 0.0)
            dst[top + i] = jnp.where(has_high, dst[top + i], 0.0)

    sweep(pa, pb, 2, True)
    round_of(2)
    sweep(pb, pa, 1)

    xqs[0] = pa[3:top, 2:4, :]
    xqs[1] = pa[3:top, 4:6, :]
    for c, (dz, dx) in enumerate(CORNERS):
        z, x = 3 if dz < 0 else top - 1, 2 if dx < 0 else 5
        ds[c] = pa[z, x : x + 1, :]
    second = Exchange(e2s, e2r)
    for side, step in ((0, -1), (1, 1)):
        second.add(xqs.at[side], xqr.at[side], 0, step)
        second.add(pa.at[pl.ds(3 if step < 0 else top - 2, 2)], zqr.at[side], step, 0)
    for c, (dz, dx) in enumerate(CORNERS):
        second.add(ds.at[c], dr.at[c], dz, dx)
    second.start()
    round_of(3)

    def residual(i):
        v, total = neighbours(pa, i)
        return sv[i - 1] - CW * v + total

    def coarsen(z, carry):
        rs[z] = residual(2 * z + 3) + residual(2 * z + 4)
        return carry

    coarse = planes // 2
    lax.fori_loop(0, coarse, coarsen, 0, unroll=2)
    for copy in loads[2:]:
        copy.wait()
    wide = coarse * 8
    spec = dot3_table_first(ty, rs[...].reshape(wide, ny), ((1,), (1,)))
    spec = spec + pltpu.roll(spec, wide - 1, 1)
    slot = lax.broadcasted_iota(jnp.int32, (xy, wide), 1) % 8
    for xx in range(2):
        packed = jnp.zeros((xy, wide), jnp.float32)
        for m in range(M):
            piece = spec[m * xy : (m + 1) * xy, :]
            shift = (m - 2 - 2 * xx) % wide
            piece = pltpu.roll(piece, shift, 1) if shift else piece
            packed = jnp.where(slot == m, piece, packed)
        s1[:, xx : xx + 1, :] = packed.reshape(xy, 1, wide)

    def everyone(axis, size, mine, src_of, dst, send, recv):
        def copy_to(i):
            to = lax.rem(mine + i, size)
            return remote(src_of(to), dst.at[mine], send.at[to], recv.at[mine], {axis: to})

        def copy_from(i):
            to = lax.rem(mine + i, size)
            return remote(src_of(to), dst.at[to], send.at[to], recv.at[to], {axis: to})

        def go(i, carry):
            copy_to(i).start()
            return carry

        def done(i, carry):
            copy_from(i).wait()
            return carry

        lax.fori_loop(1, size, go, 0)
        dst[mine] = src_of(mine)[...]
        lax.fori_loop(1, size, done, 0)

    round_of(4)
    everyone("xy", xy, me, lambda to: s1.at[to], r1, a1s, a1r)
    gathered = jnp.concatenate([r1[:, 0:1, :].reshape(xy, wide), r1[:, 1:2, :].reshape(xy, wide)], axis=0)
    fz[...] = dot3(gathered.T, fx, ((1,), (0,))).reshape(coarse, M, 2 * half)

    up = lax.broadcasted_iota(jnp.int32, (M, 2 * half), 1) < half
    theta = th[...]
    decay = jnp.exp(-theta)
    state = jnp.zeros((M, 2 * half), jnp.float32)
    for t in range(coarse):
        state = decay * state + jnp.where(up, fz[t], fz[coarse - 1 - t])
        wz[t] = state
    ztile[...] = state
    everyone("gz", gz, q, lambda to: ztile, zr, gs, gr)
    slab = jnp.exp(-float(coarse) * theta)
    total = jnp.zeros((M, 2 * half), jnp.float32)
    inflow = jnp.zeros((M, 2 * half), jnp.float32)
    steps_in = jnp.where(up, q, gz - 1 - q)
    for t in range(gz):
        inflow = jnp.where(steps_in == t, total, inflow)
        total = slab * total + jnp.where(up, zr[t], zr[gz - 1 - t])
    span = float(coarse * gz + 1)
    image = pltpu.roll(total, half, 1) - jnp.exp(-span * theta) * total
    image = image * jnp.exp(-theta * (float(coarse) * steps_in.astype(jnp.float32) + 1.0))
    inflow = inflow - image / (1.0 - jnp.exp(-2.0 * span * theta))
    scale = 1.0 / (jnp.exp(theta) - decay)
    power = decay
    for t in range(coarse):
        wz[t] = wz[t] + power * inflow
        power = power * decay
    last = decay * wz[coarse - 1]
    beyond = scale * (last + pltpu.roll(inflow, half, 1))
    above, below = jnp.where(has_high, beyond, 0.0), jnp.where(has_low, beyond, 0.0)
    above = pltpu.roll(above, half, 1)
    for z in range(coarse):
        value = scale * (wz[z] + pltpu.roll(wz[coarse - 1 - z], half, 1) - fz[z])
        ring = below if z == 0 else above if z == 1 else 0.0
        vz[pl.ds(z, M, stride=coarse), :] = jnp.where(up, value, ring)
    s2[...] = dot3_table_first(bx, vz[...], ((1,), (1,))).reshape(xy, 8, wide)
    everyone("xy", xy, me, lambda to: s2.at[to], r2, a2s, a2r)

    block = lax.broadcasted_iota(jnp.int32, (coarse, half * 2), 1) // xy
    for base, deep in ((0, coarse), (4, 8)):
        turned = jnp.concatenate([r2[:, base + e : base + e + 1, :].reshape(xy, wide) for e in range(4)], axis=0).T
        for e in range(4):
            for j in range(2):
                mixed = jnp.zeros((deep, 4 * xy), jnp.float32)
                for b in range(4):
                    at = (4 * j + b) * coarse
                    piece, shift = turned[at : at + deep, :], (b - e) % 4 * xy
                    piece = pltpu.roll(piece, shift, 1) if shift else piece
                    mixed = jnp.where(block[:deep] == b, piece, mixed)
                for twice in range(2):
                    row, count = (2 * e + twice, coarse) if base == 0 else (wide + 2 * e + twice, 2)
                    tm.at[j][pl.ds(row, count, stride=8), :] = mixed[:count]
    cc[...] = dot3(jnp.concatenate([tm[0], tm[1]], axis=1), ty, ((1,), (0,))).reshape(coarse + 2, 8, ny)

    second.wait()
    pa[3:top, 0:2, :] = jnp.where(has_near, xqr[1], 0.0)
    pa[3:top, 6:8, :] = jnp.where(has_far, xqr[0], 0.0)
    pa[1:3, 2:6, :] = jnp.where(has_low, zqr[1, :, 2:6, :], 0.0)
    pa[top : top + 2, 2:6, :] = jnp.where(has_high, zqr[0, :, 2:6, :], 0.0)
    for c, (dz, dx) in enumerate(CORNERS):
        z0, z1, x0, x1, there = corner_places(dz, dx)
        pa[z0, x0 : x0 + 1, :] = jnp.where(there, dr[c], 0.0)

    def lift(z, carry):
        fix = cc[z]
        pa[2 * z + 3] = pa[2 * z + 3] + fix
        pa[2 * z + 4] = pa[2 * z + 4] + fix
        return carry

    lax.fori_loop(0, coarse, lift, 0, unroll=2)
    for i, z in ((1, coarse), (2, coarse), (top, coarse + 1), (top + 1, coarse + 1)):
        pa[i] = pa[i] + cc[z]
    sweep(pa, pb, 1)

    def last_sweep(i, carry):
        out_ref[i - 3] = relax(pb, i)[2:6, :]
        return carry

    lax.fori_loop(3, top, last_sweep, 0, unroll=4)


def body(gz, xy, consts, source, potential):
    planes, rows, ny = source.shape
    coarse = planes // 2
    wide, two = coarse * 8, 4 * xy
    f32 = jnp.float32
    vm = lambda *shape: pltpu.VMEM(shape, f32)
    half = lambda *shape: pltpu.VMEM((2, *shape), jnp.bfloat16)
    dma = lambda n: pltpu.SemaphoreType.DMA((n,))
    scratch = [
        vm(planes, rows, ny), vm(planes, rows, ny), half(M * xy, ny), half(2 * xy, two), half(8 * xy, two), vm(M, two),
        vm(planes + 6, 8, ny), vm(planes + 6, 8, ny), vm(planes + 4, 8, ny),
        vm(2, planes, 2, ny), vm(2, planes, 2, ny), vm(2, planes, 1, ny), vm(2, planes + 4, 1, ny),
        vm(2, planes, 2, ny), vm(2, planes, 2, ny),
        vm(2, 3, rows, ny), vm(2, 2, rows, ny), vm(4, 4, ny), vm(4, 4, ny),
        vm(2, planes, 2, ny), vm(2, planes, 2, ny), vm(2, 2, 8, ny), vm(4, 1, ny), vm(4, 1, ny),
        vm(coarse, 8, ny), vm(xy, 2, wide), vm(xy, 2, wide), vm(coarse, M, two), vm(coarse, M, two),
        vm(M, two), vm(gz, M, two), vm(wide, two), vm(xy, 8, wide), vm(xy, 8, wide),
        vm(2, wide + 16, 4 * xy), vm(coarse + 2, 8, ny),
        dma(6), dma(14), dma(14), dma(8), dma(8), dma(xy), dma(xy), dma(gz), dma(gz), dma(xy), dma(xy),
        pltpu.SemaphoreType.REGULAR((4,)), pltpu.SemaphoreType.REGULAR((4,)),
    ]
    hbm = pl.BlockSpec(memory_space=pl.ANY)
    return pl.pallas_call(
        functools.partial(kernel, gz, xy),
        out_shape=jax.ShapeDtypeStruct(source.shape, f32),
        in_specs=[hbm] * 6,
        out_specs=pl.BlockSpec(memory_space=pltpu.VMEM),
        scratch_shapes=scratch,
        compiler_params=pltpu.CompilerParams(collective_id=0, has_side_effects=True),
        name="vcycle",
    )(source, potential, *[jnp.asarray(c) for c in consts])


def solution(mesh):
    gz, xy = mesh.shape["gz"], mesh.shape["xy"]
    consts = tables(xy)
    placed = (P("gz", "xy", None), P("gz", "xy", None))
    return jax.shard_map(
        functools.partial(body, gz, xy, consts), mesh=mesh, in_specs=placed,
        out_specs=P("gz", "xy", None), check_vma=False,
    )
```

```python
import functools
import math

import jax
import jax.numpy as jnp
import ml_dtypes
import numpy as np
from jax import lax
from jax.experimental import pallas as pl
from jax.experimental.pallas import tpu as pltpu
from jax.sharding import PartitionSpec as P

SCREEN = 64
OMEGA = 0.8
KAPPA = 1.0 / (SCREEN * SCREEN)
CW = 6.0 + KAPPA
M = 8
CORNERS = ((-1, -1), (-1, 1), (1, -1), (1, 1))


def sine(count):
    idx = np.arange(1, count + 1, dtype=np.int64)
    turns = idx[:, None] * idx[None, :] % (2 * (count + 1))
    return math.sqrt(2.0 / (count + 1)) * np.sin(math.pi / (count + 1) * turns)


def eigen(count):
    return 2.0 - 2.0 * np.cos(math.pi / (count + 1) * np.arange(1, count + 1))


def two_parts(table):
    coarse = table.astype(ml_dtypes.bfloat16)
    return np.stack([coarse, (table - coarse.astype(np.float64)).astype(ml_dtypes.bfloat16)])


def dot3(value, table, dims):
    coarse = value.astype(jnp.bfloat16)
    fine = (value - coarse.astype(jnp.float32)).astype(jnp.bfloat16)
    dot = lambda a, b: lax.dot_general(a, b, (dims, ((), ())), preferred_element_type=jnp.float32)
    return dot(coarse, table[0]) + dot(fine, table[0]) + dot(coarse, table[1])


def dot3_table_first(table, value, dims):
    coarse = value.astype(jnp.bfloat16)
    fine = (value - coarse.astype(jnp.float32)).astype(jnp.bfloat16)
    dot = lambda a, b: lax.dot_general(a, b, (dims, ((), ())), preferred_element_type=jnp.float32)
    return dot(table[0], coarse) + dot(table[0], fine) + dot(table[1], coarse)


def tables(groups):
    nx, ny = 2 * groups, M * groups
    sx, sy = sine(nx), sine(ny)
    ty = np.repeat(sy, 2, axis=1)
    order = np.concatenate([np.arange(0, nx, 2), np.arange(1, nx, 2)])
    fx = 0.5 * np.concatenate([sx[order], sx[order]], axis=1)
    bx = np.zeros((groups, 8, 2 * nx))
    for d in range(groups):
        for e in range(4):
            x = 2 * d - 1 + e
            if 0 <= x < nx:
                bx[d, e, :nx] = sx[x]
                bx[d, 4 + e, nx:] = sx[x]
    diag = 2.0 + eigen(nx)[None, None, :] + eigen(ny).reshape(M, groups).T[:, :, None] + 4.0 * KAPPA
    theta = np.arccosh(0.5 * diag)
    theta = np.concatenate([theta, theta], axis=2)
    return two_parts(ty), two_parts(fx), two_parts(bx.reshape(groups * 8, 2 * nx)), theta.astype(np.float32)


def kernel(
    gz, xy, src_hbm, pot_hbm, ty_hbm, fx_hbm, bx_hbm, th_hbm, out_hbm,
    potv, srcv, ty, fx, bx, th, pa, pb, sv,
    xps, xpr, xts, xtr, xss, xsr, zpr, zsr, cs, cr,
    xqs, xqr, zqr, ds, dr,
    rs, s1, r1, fz, wz, ztile, zr, vz, s2, r2, tm, cc,
    ld, e1s, e1r, e2s, e2r, a1s, a1r, gs, gr, a2s, a2r, outs, known_x, known_z,
):
    q, me = lax.axis_index("gz"), lax.axis_index("xy")
    planes, rows, ny = potv.shape
    half = 2 * xy
    top = planes + 3

    loads = [
        pltpu.make_async_copy(pot_hbm, potv, ld.at[0]),
        pltpu.make_async_copy(src_hbm, srcv, ld.at[1]),
        pltpu.make_async_copy(ty_hbm, ty, ld.at[2]),
        pltpu.make_async_copy(fx_hbm, fx, ld.at[3]),
        pltpu.make_async_copy(bx_hbm, bx, ld.at[4]),
        pltpu.make_async_copy(th_hbm.at[me], th, ld.at[5]),
    ]
    def shifted(dz, dx):
        where = {}
        if dz:
            where["gz"] = lax.rem(q + dz + gz, gz)
        if dx:
            where["xy"] = lax.rem(me + dx + xy, xy)
        return where

    def tell(sem, where):
        pl.semaphore_signal(sem, inc=1, device_id=where, device_id_type=pl.DeviceIdType.MESH)

    barrier = pltpu.get_barrier_semaphore()
    for dz, dx in CORNERS + ((-1, 0), (1, 0), (0, -1), (0, 1)):
        tell(barrier, shifted(dz, dx))
    loads[0].start()
    loads[1].start()

    pa[...] = jnp.zeros_like(pa)
    sv[...] = jnp.zeros_like(sv)
    for side in range(2):
        xtr[side, 0:2] = jnp.zeros((2, 1, ny), jnp.float32)
        xtr[side, planes + 2 : planes + 4] = jnp.zeros((2, 1, ny), jnp.float32)
    loads[0].wait()
    loads[1].wait()
    xps[0] = potv[:, 0:2, :]
    xps[1] = potv[:, 2:4, :]
    xts[0] = potv[:, 2:3, :]
    xts[1] = potv[:, 1:2, :]
    xss[0] = srcv[:, 0:2, :]
    xss[1] = srcv[:, 2:4, :]
    for c, (dz, dx) in enumerate(CORNERS):
        z0, z1 = (0, 1) if dz < 0 else (planes - 1, planes - 2)
        x0, x1 = (0, 1) if dx < 0 else (rows - 1, rows - 2)
        cs[c, 0:1] = potv[z0, x0 : x0 + 1, :]
        cs[c, 1:2] = potv[z0, x1 : x1 + 1, :]
        cs[c, 2:3] = potv[z1, x0 : x0 + 1, :]
        cs[c, 3:4] = srcv[z0, x0 : x0 + 1, :]
    pl.semaphore_wait(barrier, 8)

    def round_of(level):
        for axis, size, dim, known in (("xy", xy, 1, known_x), ("gz", gz, 0, known_z)):
            reach = 2**level
            if level and reach // 2 < size // 2:
                pl.semaphore_wait(known.at[level - 1], 2)
            if reach < size // 2:
                for way in (-reach, reach):
                    tell(known.at[level], shifted(way, 0) if dim == 0 else shifted(0, way))

    round_of(0)

    class Exchange:
        def __init__(self, send, recv):
            self.send, self.recv, self.copies = send, recv, []

        def add(self, src, dst, dz, dx):
            slot = len(self.copies)
            copy = remote(src, dst, self.send.at[slot], self.recv.at[slot], shifted(dz, dx))
            self.copies.append((copy, exists(dz, dx), exists(-dz, -dx)))

        def start(self, slot):
            copy, there, unused = self.copies[slot]
            pl.when(there)(copy.start)

        def wait(self):
            for copy, there, back in self.copies:
                pl.when(back)(copy.wait_recv)
                pl.when(there)(copy.wait_send)

    def exists(dz, dx):
        there = None
        for step, mine, size in ((dz, q, gz), (dx, me, xy)):
            if step:
                ok = mine > 0 if step < 0 else mine < size - 1
                there = ok if there is None else jnp.logical_and(there, ok)
        return there

    def remote(src, dst, send, recv, where):
        return pltpu.make_async_remote_copy(
            src_ref=src, dst_ref=dst, send_sem=send, recv_sem=recv,
            device_id=where, device_id_type=pl.DeviceIdType.MESH,
        )

    first = Exchange(e1s, e1r)
    for side, step in ((0, -1), (1, 1)):
        first.add(xps.at[side], xpr.at[side], 0, step)
        first.add(xts.at[side], xtr.at[side, pl.ds(2, planes)], 0, step)
        first.add(xss.at[side], xsr.at[side], 0, step)
        first.add(potv.at[pl.ds(0 if step < 0 else planes - 3, 3)], zpr.at[side], step, 0)
        first.add(srcv.at[pl.ds(0 if step < 0 else planes - 2, 2)], zsr.at[side], step, 0)
    for c, (dz, dx) in enumerate(CORNERS):
        first.add(cs.at[c], cr.at[c], dz, dx)
    for slot in range(len(first.copies)):
        first.start(slot)
    for copy in loads[2:]:
        copy.start()

    pa[3:top, 2:6, :] = potv[...]
    sv[2 : planes + 2, 2:6, :] = srcv[...]
    sub = lax.broadcasted_iota(jnp.int32, (8, ny), 0)
    lane = lax.broadcasted_iota(jnp.int32, (8, ny), 1)
    inside = jnp.logical_and(
        jnp.logical_or(sub >= 2, me > 0), jnp.logical_or(sub < 6, me < xy - 1)
    )
    has_low, has_high, has_near, has_far = q > 0, q < gz - 1, me > 0, me < xy - 1

    def corner_places(dz, dx):
        z0, z1 = (top, top + 1) if dz < 0 else (2, 1)
        x0, x1 = (6, 7) if dx < 0 else (1, 0)
        return z0, z1, x0, x1, exists(-dz, -dx)

    round_of(1)
    round_of(2)
    first.wait()
    round_of(3)
    pa[3:top, 0:2, :] = jnp.where(has_near, xpr[1], 0.0)
    pa[3:top, 6:8, :] = jnp.where(has_far, xpr[0], 0.0)
    pa[0:3, 2:6, :] = jnp.where(has_low, zpr[1], 0.0)
    pa[top : top + 3, 2:6, :] = jnp.where(has_high, zpr[0], 0.0)
    sv[2 : planes + 2, 0:2, :] = jnp.where(has_near, xsr[1], 0.0)
    sv[2 : planes + 2, 6:8, :] = jnp.where(has_far, xsr[0], 0.0)
    sv[0:2, 2:6, :] = jnp.where(has_low, zsr[1], 0.0)
    sv[planes + 2 : planes + 4, 2:6, :] = jnp.where(has_high, zsr[0], 0.0)
    for c, (dz, dx) in enumerate(CORNERS):
        z0, z1, x0, x1, there = corner_places(dz, dx)
        corner = jnp.where(there, cr[c], 0.0)
        pa[z0, x0 : x0 + 1, :] = corner[0:1]
        pa[z0, x1 : x1 + 1, :] = corner[1:2]
        pa[z1, x0 : x0 + 1, :] = corner[2:3]
        sv[z0 - 1, x0 : x0 + 1, :] = corner[3:4]

    def neighbours(ref, i, ends=None):
        v = ref[i]
        total = ref[i - 1] + ref[i + 1]
        back, forth = pltpu.roll(v, 1, 0), pltpu.roll(v, 7, 0)
        if ends is not None:
            back, forth = jnp.where(sub == 0, ends[0], back), jnp.where(sub == 7, ends[1], forth)
        total = total + back + forth
        total = total + jnp.where(lane == 0, 0.0, pltpu.roll(v, 1, 1))
        total = total + jnp.where(lane == ny - 1, 0.0, pltpu.roll(v, ny - 1, 1))
        return v, total

    def relax(ref, i, ends=None):
        v, total = neighbours(ref, i, ends)
        return (1.0 - OMEGA) * v + (OMEGA / CW) * (sv[i - 1] + total)

    def sweep(src, dst, ring, ended=False):
        def step(i, carry):
            ends = None
            if ended:
                ends = [jnp.where(there, xtr[side, i - 1], 0.0) for there, side in ((has_near, 1), (has_far, 0))]
            dst[i] = jnp.where(inside, relax(src, i, ends), 0.0)
            return carry

        if ring == 2:
            lax.fori_loop(1, top + 2, step, 0, unroll=4)
        else:
            lax.fori_loop(3, top, step, 0, unroll=4)
            step(2, 0)
            step(top, 0)
        for i in range(ring):
            dst[2 - i] = jnp.where(has_low, dst[2 - i], 0.0)
            dst[top + i] = jnp.where(has_high, dst[top + i], 0.0)

    sweep(pa, pb, 2, True)
    sweep(pb, pa, 1)
    round_of(4)

    xqs[0] = pa[3:top, 2:4, :]
    xqs[1] = pa[3:top, 4:6, :]
    for c, (dz, dx) in enumerate(CORNERS):
        z, x = 3 if dz < 0 else top - 1, 2 if dx < 0 else 5
        ds[c] = pa[z, x : x + 1, :]
    second = Exchange(e2s, e2r)
    for side, step in ((0, -1), (1, 1)):
        second.add(xqs.at[side], xqr.at[side], 0, step)
        second.add(pa.at[pl.ds(3 if step < 0 else top - 2, 2)], zqr.at[side], step, 0)
    for c, (dz, dx) in enumerate(CORNERS):
        second.add(ds.at[c], dr.at[c], dz, dx)
    for slot in (1, 3, 4, 5, 6, 7):
        second.start(slot)

    def residual(i):
        v, total = neighbours(pa, i)
        return sv[i - 1] - CW * v + total

    def coarsen(z, carry):
        rs[z] = residual(2 * z + 3) + residual(2 * z + 4)
        return carry

    coarse = planes // 2
    lax.fori_loop(0, coarse, coarsen, 0, unroll=2)
    for copy in loads[2:]:
        copy.wait()
    wide = coarse * 8
    spec = dot3_table_first(ty, rs[...].reshape(wide, ny), ((1,), (1,)))
    spec = spec + pltpu.roll(spec, wide - 1, 1)
    slot = lax.broadcasted_iota(jnp.int32, (xy, wide), 1) % 8
    for xx in range(2):
        packed = jnp.zeros((xy, wide), jnp.float32)
        for m in range(M):
            piece = spec[m * xy : (m + 1) * xy, :]
            shift = (m - 2 - 2 * xx) % wide
            piece = pltpu.roll(piece, shift, 1) if shift else piece
            packed = jnp.where(slot == m, piece, packed)
        s1[:, xx : xx + 1, :] = packed.reshape(xy, 1, wide)

    def everyone(axis, size, mine, far, src_of, dst, send, recv):
        for i in sorted(range(1, size), key=far, reverse=True):
            to = lax.rem(mine + i, size)
            remote(src_of(to), dst.at[mine], send.at[0], recv.at[0], {axis: to}).start()
        dst[mine] = src_of(mine)[...]
        rest = dst.at[pl.ds(0, size - 1)]
        done = remote(rest, rest, send.at[0], recv.at[0], {axis: lax.rem(mine + 1, size)})
        done.wait_recv()
        done.wait_send()

    def hops_xy(i):
        return min(i // 8, 4 - i // 8) + min(i % 8 // 2, 4 - i % 8 // 2)

    def hops_z(i):
        return min(i, gz - i)

    everyone("xy", xy, me, hops_xy, lambda to: s1.at[to], r1, a1s, a1r)
    second.start(0)
    second.start(2)
    gathered = jnp.concatenate([r1[:, 0:1, :].reshape(xy, wide), r1[:, 1:2, :].reshape(xy, wide)], axis=0)
    fz[...] = dot3(gathered.T, fx, ((1,), (0,))).reshape(coarse, M, 2 * half)

    up = lax.broadcasted_iota(jnp.int32, (M, 2 * half), 1) < half
    theta = th[...]
    decay = jnp.exp(-theta)
    state = jnp.zeros((M, 2 * half), jnp.float32)
    for t in range(coarse):
        state = decay * state + jnp.where(up, fz[t], fz[coarse - 1 - t])
        wz[t] = state
    ztile[...] = state
    everyone("gz", gz, q, hops_z, lambda to: ztile, zr, gs, gr)
    slab = jnp.exp(-float(coarse) * theta)
    total = jnp.zeros((M, 2 * half), jnp.float32)
    inflow = jnp.zeros((M, 2 * half), jnp.float32)
    steps_in = jnp.where(up, q, gz - 1 - q)
    for t in range(gz):
        inflow = jnp.where(steps_in == t, total, inflow)
        total = slab * total + jnp.where(up, zr[t], zr[gz - 1 - t])
    span = float(coarse * gz + 1)
    image = pltpu.roll(total, half, 1) - jnp.exp(-span * theta) * total
    image = image * jnp.exp(-theta * (float(coarse) * steps_in.astype(jnp.float32) + 1.0))
    inflow = inflow - image / (1.0 - jnp.exp(-2.0 * span * theta))
    scale = 1.0 / (jnp.exp(theta) - decay)
    power = decay
    for t in range(coarse):
        wz[t] = wz[t] + power * inflow
        power = power * decay
    last = decay * wz[coarse - 1]
    beyond = scale * (last + pltpu.roll(inflow, half, 1))
    above, below = jnp.where(has_high, beyond, 0.0), jnp.where(has_low, beyond, 0.0)
    above = pltpu.roll(above, half, 1)
    for z in range(coarse):
        value = scale * (wz[z] + pltpu.roll(wz[coarse - 1 - z], half, 1) - fz[z])
        ring = below if z == 0 else above if z == 1 else 0.0
        vz[pl.ds(z, M, stride=coarse), :] = jnp.where(up, value, ring)
    s2[...] = dot3_table_first(bx, vz[...], ((1,), (1,))).reshape(xy, 8, wide)
    everyone("xy", xy, me, hops_xy, lambda to: s2.at[to], r2, a2s, a2r)

    block = lax.broadcasted_iota(jnp.int32, (coarse, half * 2), 1) // xy
    for base, deep in ((0, coarse), (4, 8)):
        turned = jnp.concatenate([r2[:, base + e : base + e + 1, :].reshape(xy, wide) for e in range(4)], axis=0).T
        for e in range(4):
            for j in range(2):
                mixed = jnp.zeros((deep, 4 * xy), jnp.float32)
                for b in range(4):
                    at = (4 * j + b) * coarse
                    piece, shift = turned[at : at + deep, :], (b - e) % 4 * xy
                    piece = pltpu.roll(piece, shift, 1) if shift else piece
                    mixed = jnp.where(block[:deep] == b, piece, mixed)
                for twice in range(2):
                    row, count = (2 * e + twice, coarse) if base == 0 else (wide + 2 * e + twice, 2)
                    tm.at[j][pl.ds(row, count, stride=8), :] = mixed[:count]
    cc[...] = dot3(jnp.concatenate([tm[0], tm[1]], axis=1), ty, ((1,), (0,))).reshape(coarse + 2, 8, ny)

    second.wait()
    pa[3:top, 0:2, :] = jnp.where(has_near, xqr[1], 0.0)
    pa[3:top, 6:8, :] = jnp.where(has_far, xqr[0], 0.0)
    pa[1:3, 2:6, :] = jnp.where(has_low, zqr[1, :, 2:6, :], 0.0)
    pa[top : top + 2, 2:6, :] = jnp.where(has_high, zqr[0, :, 2:6, :], 0.0)
    for c, (dz, dx) in enumerate(CORNERS):
        z0, z1, x0, x1, there = corner_places(dz, dx)
        pa[z0, x0 : x0 + 1, :] = jnp.where(there, dr[c], 0.0)

    def lift(z, carry):
        fix = cc[z]
        pa[2 * z + 3] = pa[2 * z + 3] + fix
        pa[2 * z + 4] = pa[2 * z + 4] + fix
        return carry

    lax.fori_loop(0, coarse, lift, 0, unroll=2)
    for i, z in ((1, coarse), (2, coarse), (top, coarse + 1), (top + 1, coarse + 1)):
        pa[i] = pa[i] + cc[z]
    sweep(pa, pb, 1)

    def last_sweep(i, carry):
        potv[i - 3] = relax(pb, i)[2:6, :]
        return carry

    part = planes // 4
    leaving = []
    for c in range(4):
        lax.fori_loop(3 + c * part, 3 + (c + 1) * part, last_sweep, 0, unroll=4)
        here = pl.ds(c * part, part)
        leaving.append(pltpu.make_async_copy(potv.at[here], out_hbm.at[here], outs.at[c]))
        leaving[-1].start()
    for copy in leaving:
        copy.wait()


def body(gz, xy, consts, source, potential):
    planes, rows, ny = source.shape
    coarse = planes // 2
    wide, two = coarse * 8, 4 * xy
    f32 = jnp.float32
    vm = lambda *shape: pltpu.VMEM(shape, f32)
    half = lambda *shape: pltpu.VMEM((2, *shape), jnp.bfloat16)
    dma = lambda n: pltpu.SemaphoreType.DMA((n,))
    scratch = [
        vm(planes, rows, ny), vm(planes, rows, ny), half(M * xy, ny), half(2 * xy, two), half(8 * xy, two), vm(M, two),
        vm(planes + 6, 8, ny), vm(planes + 6, 8, ny), vm(planes + 4, 8, ny),
        vm(2, planes, 2, ny), vm(2, planes, 2, ny), vm(2, planes, 1, ny), vm(2, planes + 4, 1, ny),
        vm(2, planes, 2, ny), vm(2, planes, 2, ny),
        vm(2, 3, rows, ny), vm(2, 2, rows, ny), vm(4, 4, ny), vm(4, 4, ny),
        vm(2, planes, 2, ny), vm(2, planes, 2, ny), vm(2, 2, 8, ny), vm(4, 1, ny), vm(4, 1, ny),
        vm(coarse, 8, ny), vm(xy, 2, wide), vm(xy, 2, wide), vm(coarse, M, two), vm(coarse, M, two),
        vm(M, two), vm(gz, M, two), vm(wide, two), vm(xy, 8, wide), vm(xy, 8, wide),
        vm(2, wide + 16, 4 * xy), vm(coarse + 2, 8, ny),
        dma(6), dma(14), dma(14), dma(8), dma(8), dma(1), dma(1), dma(1), dma(1), dma(1), dma(1), dma(4),
        pltpu.SemaphoreType.REGULAR((4,)), pltpu.SemaphoreType.REGULAR((4,)),
    ]
    hbm = pl.BlockSpec(memory_space=pl.ANY)
    return pl.pallas_call(
        functools.partial(kernel, gz, xy),
        out_shape=jax.ShapeDtypeStruct(source.shape, f32),
        in_specs=[pl.BlockSpec(memory_space=pltpu.HBM)] * 6,
        out_specs=hbm,
        scratch_shapes=scratch,
        compiler_params=pltpu.CompilerParams(vmem_limit_bytes=24 * 1024 * 1024, collective_id=0, has_side_effects=True),
        name="vcycle",
    )(*[pltpu.with_memory_space_constraint(a, pltpu.HBM) for a in (source, potential, *map(jnp.asarray, consts))])


def solution(mesh):
    gz, xy = mesh.shape["gz"], mesh.shape["xy"]
    consts = tables(xy)
    placed = (P("gz", "xy", None), P("gz", "xy", None))
    return jax.shard_map(
        functools.partial(body, gz, xy, consts), mesh=mesh, in_specs=placed,
        out_specs=P("gz", "xy", None), check_vma=False,
    )
```

```python
import functools
import math

import jax
import jax.numpy as jnp
import ml_dtypes
import numpy as np
from jax import lax
from jax.experimental import pallas as pl
from jax.experimental.pallas import tpu as pltpu
from jax.sharding import PartitionSpec as P

SCREEN = 64
OMEGA = 0.8
KAPPA = 1.0 / (SCREEN * SCREEN)
CW = 6.0 + KAPPA
M = 8
CORNERS = ((-1, -1), (-1, 1), (1, -1), (1, 1))


def sine(count):
    idx = np.arange(1, count + 1, dtype=np.int64)
    turns = idx[:, None] * idx[None, :] % (2 * (count + 1))
    return math.sqrt(2.0 / (count + 1)) * np.sin(math.pi / (count + 1) * turns)


def eigen(count):
    return 2.0 - 2.0 * np.cos(math.pi / (count + 1) * np.arange(1, count + 1))


def two_parts(table):
    coarse = table.astype(ml_dtypes.bfloat16)
    return np.stack([coarse, (table - coarse.astype(np.float64)).astype(ml_dtypes.bfloat16)])


def dot3(value, table, dims):
    coarse = value.astype(jnp.bfloat16)
    fine = (value - coarse.astype(jnp.float32)).astype(jnp.bfloat16)
    dot = lambda a, b: lax.dot_general(a, b, (dims, ((), ())), preferred_element_type=jnp.float32)
    return dot(coarse, table[0]) + dot(fine, table[0]) + dot(coarse, table[1])


def dot3_table_first(table, value, dims):
    coarse = value.astype(jnp.bfloat16)
    fine = (value - coarse.astype(jnp.float32)).astype(jnp.bfloat16)
    dot = lambda a, b: lax.dot_general(a, b, (dims, ((), ())), preferred_element_type=jnp.float32)
    return dot(table[0], coarse) + dot(table[0], fine) + dot(table[1], coarse)


def tables(groups):
    nx, ny = 2 * groups, M * groups
    sx, sy = sine(nx), sine(ny)
    ty = np.repeat(sy, 2, axis=1)
    order = np.concatenate([np.arange(0, nx, 2), np.arange(1, nx, 2)])
    fx = 0.5 * np.concatenate([sx[order], sx[order]], axis=1)
    bx = np.zeros((groups, 8, 2 * nx))
    for d in range(groups):
        for e in range(4):
            x = 2 * d - 1 + e
            if 0 <= x < nx:
                bx[d, e, :nx] = sx[x]
                bx[d, 4 + e, nx:] = sx[x]
    diag = 2.0 + eigen(nx)[None, None, :] + eigen(ny).reshape(M, groups).T[:, :, None] + 4.0 * KAPPA
    theta = np.arccosh(0.5 * diag)
    theta = np.concatenate([theta, theta], axis=2)
    return two_parts(ty), two_parts(fx), two_parts(bx.reshape(groups * 8, 2 * nx)), theta.astype(np.float32)


def kernel(
    gz, xy, src_hbm, pot_hbm, ty_hbm, fx_hbm, bx_hbm, th_hbm, out_hbm,
    potv, srcv, ty, fx, bx, th, pa, pb, sv,
    xps, xpr, xts, xtr, xss, xsr, zpr, zsr, cs, cr,
    xqs, xqr, zqr, ds, dr,
    rs, s1, r1, fz, wz, ztile, zr, vz, s2, r2, tm, cc,
    ld, e1s, e1r, e2s, e2r, a1s, a1r, gs, gr, a2s, a2r, outs, known_x, known_z,
):
    q, me = lax.axis_index("gz"), lax.axis_index("xy")
    planes, rows, ny = potv.shape
    half = 2 * xy
    top = planes + 3

    loads = [
        pltpu.make_async_copy(pot_hbm, potv, ld.at[0]),
        pltpu.make_async_copy(src_hbm, srcv, ld.at[1]),
        pltpu.make_async_copy(ty_hbm, ty, ld.at[2]),
        pltpu.make_async_copy(fx_hbm, fx, ld.at[3]),
        pltpu.make_async_copy(bx_hbm, bx, ld.at[4]),
        pltpu.make_async_copy(th_hbm.at[me], th, ld.at[5]),
    ]
    def shifted(dz, dx):
        where = {}
        if dz:
            where["gz"] = lax.rem(q + dz + gz, gz)
        if dx:
            where["xy"] = lax.rem(me + dx + xy, xy)
        return where

    def tell(sem, where):
        pl.semaphore_signal(sem, inc=1, device_id=where, device_id_type=pl.DeviceIdType.MESH)

    barrier = pltpu.get_barrier_semaphore()
    for dz, dx in CORNERS + ((-1, 0), (1, 0), (0, -1), (0, 1)):
        tell(barrier, shifted(dz, dx))
    loads[0].start()
    loads[1].start()

    for side in range(2):
        xtr[side, 0:2] = jnp.zeros((2, 1, ny), jnp.float32)
        xtr[side, planes + 2 : planes + 4] = jnp.zeros((2, 1, ny), jnp.float32)
    loads[0].wait()
    xps[0] = potv[:, 0:2, :]
    xps[1] = potv[:, 2:4, :]
    xts[0] = potv[:, 2:3, :]
    xts[1] = potv[:, 1:2, :]
    pl.semaphore_wait(barrier, 8)

    def round_of(level):
        for axis, size, dim, known in (("xy", xy, 1, known_x), ("gz", gz, 0, known_z)):
            reach = 2**level
            if level and reach // 2 < size // 2:
                pl.semaphore_wait(known.at[level - 1], 2)
            if reach < size // 2:
                for way in (-reach, reach):
                    tell(known.at[level], shifted(way, 0) if dim == 0 else shifted(0, way))

    class Exchange:
        def __init__(self, send, recv):
            self.send, self.recv, self.copies = send, recv, []

        def add(self, src, dst, dz, dx):
            slot = len(self.copies)
            copy = remote(src, dst, self.send.at[slot], self.recv.at[slot], shifted(dz, dx))
            self.copies.append((copy, exists(dz, dx), exists(-dz, -dx)))

        def start(self, slot):
            copy, there, unused = self.copies[slot]
            pl.when(there)(copy.start)

        def wait(self):
            for copy, there, back in self.copies:
                pl.when(back)(copy.wait_recv)
                pl.when(there)(copy.wait_send)

    def exists(dz, dx):
        there = None
        for step, mine, size in ((dz, q, gz), (dx, me, xy)):
            if step:
                ok = mine > 0 if step < 0 else mine < size - 1
                there = ok if there is None else jnp.logical_and(there, ok)
        return there

    def remote(src, dst, send, recv, where):
        return pltpu.make_async_remote_copy(
            src_ref=src, dst_ref=dst, send_sem=send, recv_sem=recv,
            device_id=where, device_id_type=pl.DeviceIdType.MESH,
        )

    first = Exchange(e1s, e1r)
    for side, step in ((0, -1), (1, 1)):
        first.add(xps.at[side], xpr.at[side], 0, step)
        first.add(xts.at[side], xtr.at[side, pl.ds(2, planes)], 0, step)
        first.add(xss.at[side], xsr.at[side], 0, step)
        first.add(potv.at[pl.ds(0 if step < 0 else planes - 3, 3)], zpr.at[side], step, 0)
        first.add(srcv.at[pl.ds(0 if step < 0 else planes - 2, 2)], zsr.at[side], step, 0)
    for c, (dz, dx) in enumerate(CORNERS):
        first.add(cs.at[c], cr.at[c], dz, dx)
    for slot in (0, 5, 1, 6, 3, 8):
        first.start(slot)
    round_of(0)
    loads[1].wait()
    xss[0] = srcv[:, 0:2, :]
    xss[1] = srcv[:, 2:4, :]
    for c, (dz, dx) in enumerate(CORNERS):
        z0, z1 = (0, 1) if dz < 0 else (planes - 1, planes - 2)
        x0, x1 = (0, 1) if dx < 0 else (rows - 1, rows - 2)
        cs[c, 0:1] = potv[z0, x0 : x0 + 1, :]
        cs[c, 1:2] = potv[z0, x1 : x1 + 1, :]
        cs[c, 2:3] = potv[z1, x0 : x0 + 1, :]
        cs[c, 3:4] = srcv[z0, x0 : x0 + 1, :]
    for slot in (2, 7, 4, 9, 10, 11, 12, 13):
        first.start(slot)
    for copy in loads[2:]:
        copy.start()

    pa[...] = jnp.zeros_like(pa)
    sv[...] = jnp.zeros_like(sv)
    pa[3:top, 2:6, :] = potv[...]
    sv[2 : planes + 2, 2:6, :] = srcv[...]
    sub = lax.broadcasted_iota(jnp.int32, (8, ny), 0)
    lane = lax.broadcasted_iota(jnp.int32, (8, ny), 1)
    inside = jnp.logical_and(
        jnp.logical_or(sub >= 2, me > 0), jnp.logical_or(sub < 6, me < xy - 1)
    )
    has_low, has_high, has_near, has_far = q > 0, q < gz - 1, me > 0, me < xy - 1

    def corner_places(dz, dx):
        z0, z1 = (top, top + 1) if dz < 0 else (2, 1)
        x0, x1 = (6, 7) if dx < 0 else (1, 0)
        return z0, z1, x0, x1, exists(-dz, -dx)

    round_of(1)
    round_of(2)
    first.wait()
    round_of(3)
    pa[3:top, 0:2, :] = jnp.where(has_near, xpr[1], 0.0)
    pa[3:top, 6:8, :] = jnp.where(has_far, xpr[0], 0.0)
    pa[0:3, 2:6, :] = jnp.where(has_low, zpr[1], 0.0)
    pa[top : top + 3, 2:6, :] = jnp.where(has_high, zpr[0], 0.0)
    sv[2 : planes + 2, 0:2, :] = jnp.where(has_near, xsr[1], 0.0)
    sv[2 : planes + 2, 6:8, :] = jnp.where(has_far, xsr[0], 0.0)
    sv[0:2, 2:6, :] = jnp.where(has_low, zsr[1], 0.0)
    sv[planes + 2 : planes + 4, 2:6, :] = jnp.where(has_high, zsr[0], 0.0)
    for c, (dz, dx) in enumerate(CORNERS):
        z0, z1, x0, x1, there = corner_places(dz, dx)
        corner = jnp.where(there, cr[c], 0.0)
        pa[z0, x0 : x0 + 1, :] = corner[0:1]
        pa[z0, x1 : x1 + 1, :] = corner[1:2]
        pa[z1, x0 : x0 + 1, :] = corner[2:3]
        sv[z0 - 1, x0 : x0 + 1, :] = corner[3:4]

    def neighbours(ref, i, ends=None):
        v = ref[i]
        total = ref[i - 1] + ref[i + 1]
        back, forth = pltpu.roll(v, 1, 0), pltpu.roll(v, 7, 0)
        if ends is not None:
            back, forth = jnp.where(sub == 0, ends[0], back), jnp.where(sub == 7, ends[1], forth)
        total = total + back + forth
        total = total + jnp.where(lane == 0, 0.0, pltpu.roll(v, 1, 1))
        total = total + jnp.where(lane == ny - 1, 0.0, pltpu.roll(v, ny - 1, 1))
        return v, total

    def relax(ref, i, ends=None):
        v, total = neighbours(ref, i, ends)
        return (1.0 - OMEGA) * v + (OMEGA / CW) * (sv[i - 1] + total)

    def sweep(src, dst, ring, ended=False):
        def step(i, carry):
            ends = None
            if ended:
                ends = [jnp.where(there, xtr[side, i - 1], 0.0) for there, side in ((has_near, 1), (has_far, 0))]
            dst[i] = jnp.where(inside, relax(src, i, ends), 0.0)
            return carry

        if ring == 2:
            lax.fori_loop(1, top + 2, step, 0, unroll=4)
        else:
            lax.fori_loop(3, top, step, 0, unroll=4)
            step(2, 0)
            step(top, 0)
        for i in range(ring):
            dst[2 - i] = jnp.where(has_low, dst[2 - i], 0.0)
            dst[top + i] = jnp.where(has_high, dst[top + i], 0.0)

    sweep(pa, pb, 2, True)
    sweep(pb, pa, 1)
    round_of(4)

    xqs[0] = pa[3:top, 2:4, :]
    xqs[1] = pa[3:top, 4:6, :]
    for c, (dz, dx) in enumerate(CORNERS):
        z, x = 3 if dz < 0 else top - 1, 2 if dx < 0 else 5
        ds[c] = pa[z, x : x + 1, :]
    second = Exchange(e2s, e2r)
    for side, step in ((0, -1), (1, 1)):
        second.add(xqs.at[side], xqr.at[side], 0, step)
        second.add(pa.at[pl.ds(3 if step < 0 else top - 2, 2)], zqr.at[side], step, 0)
    for c, (dz, dx) in enumerate(CORNERS):
        second.add(ds.at[c], dr.at[c], dz, dx)
    for slot in (1, 3, 4, 5, 6, 7):
        second.start(slot)

    def residual(i):
        v, total = neighbours(pa, i)
        return sv[i - 1] - CW * v + total

    def coarsen(z, carry):
        rs[z] = residual(2 * z + 3) + residual(2 * z + 4)
        return carry

    coarse = planes // 2
    lax.fori_loop(0, coarse, coarsen, 0, unroll=2)
    for copy in loads[2:]:
        copy.wait()
    wide = coarse * 8
    spec = dot3_table_first(ty, rs[...].reshape(wide, ny), ((1,), (1,)))
    spec = spec + pltpu.roll(spec, wide - 1, 1)
    slot = lax.broadcasted_iota(jnp.int32, (xy, wide), 1) % 8
    for xx in range(2):
        packed = jnp.zeros((xy, wide), jnp.float32)
        for m in range(M):
            piece = spec[m * xy : (m + 1) * xy, :]
            shift = (m - 2 - 2 * xx) % wide
            piece = pltpu.roll(piece, shift, 1) if shift else piece
            packed = jnp.where(slot == m, piece, packed)
        s1[:, xx : xx + 1, :] = packed.reshape(xy, 1, wide)

    def everyone(axis, size, mine, far, src_of, dst, send, recv, meanwhile=None):
        for i in sorted(range(1, size), key=far, reverse=True):
            to = lax.rem(mine + i, size)
            remote(src_of(to), dst.at[mine], send.at[0], recv.at[0], {axis: to}).start()
        dst[mine] = src_of(mine)[...]
        if meanwhile is not None:
            meanwhile()
        rest = dst.at[pl.ds(0, size - 1)]
        done = remote(rest, rest, send.at[0], recv.at[0], {axis: lax.rem(mine + 1, size)})
        done.wait_recv()
        done.wait_send()

    def hops_xy(i):
        return min(i // 8, 4 - i // 8) + min(i % 8 // 2, 4 - i % 8 // 2)

    def hops_z(i):
        return min(i, gz - i)

    everyone("xy", xy, me, hops_xy, lambda to: s1.at[to], r1, a1s, a1r)
    second.start(0)
    second.start(2)
    gathered = jnp.concatenate([r1[:, 0:1, :].reshape(xy, wide), r1[:, 1:2, :].reshape(xy, wide)], axis=0)
    fz[...] = dot3(gathered.T, fx, ((1,), (0,))).reshape(coarse, M, 2 * half)

    up = lax.broadcasted_iota(jnp.int32, (M, 2 * half), 1) < half
    theta = th[...]
    decay = jnp.exp(-theta)
    state = jnp.zeros((M, 2 * half), jnp.float32)
    for t in range(coarse):
        state = decay * state + jnp.where(up, fz[t], fz[coarse - 1 - t])
        wz[t] = state
    ztile[...] = state
    everyone("gz", gz, q, hops_z, lambda to: ztile, zr, gs, gr)
    slab = jnp.exp(-float(coarse) * theta)
    total = jnp.zeros((M, 2 * half), jnp.float32)
    inflow = jnp.zeros((M, 2 * half), jnp.float32)
    steps_in = jnp.where(up, q, gz - 1 - q)
    for t in range(gz):
        inflow = jnp.where(steps_in == t, total, inflow)
        total = slab * total + jnp.where(up, zr[t], zr[gz - 1 - t])
    span = float(coarse * gz + 1)
    image = pltpu.roll(total, half, 1) - jnp.exp(-span * theta) * total
    image = image * jnp.exp(-theta * (float(coarse) * steps_in.astype(jnp.float32) + 1.0))
    inflow = inflow - image / (1.0 - jnp.exp(-2.0 * span * theta))
    scale = 1.0 / (jnp.exp(theta) - decay)
    power = decay
    for t in range(coarse):
        wz[t] = wz[t] + power * inflow
        power = power * decay
    last = decay * wz[coarse - 1]
    beyond = scale * (last + pltpu.roll(inflow, half, 1))
    above, below = jnp.where(has_high, beyond, 0.0), jnp.where(has_low, beyond, 0.0)
    above = pltpu.roll(above, half, 1)
    for z in range(coarse):
        value = scale * (wz[z] + pltpu.roll(wz[coarse - 1 - z], half, 1) - fz[z])
        ring = below if z == 0 else above if z == 1 else 0.0
        vz[pl.ds(z, M, stride=coarse), :] = jnp.where(up, value, ring)
    s2[...] = dot3_table_first(bx, vz[...], ((1,), (1,))).reshape(xy, 8, wide)
    def second_halo():
        second.wait()
        pa[3:top, 0:2, :] = jnp.where(has_near, xqr[1], 0.0)
        pa[3:top, 6:8, :] = jnp.where(has_far, xqr[0], 0.0)
        pa[1:3, 2:6, :] = jnp.where(has_low, zqr[1, :, 2:6, :], 0.0)
        pa[top : top + 2, 2:6, :] = jnp.where(has_high, zqr[0, :, 2:6, :], 0.0)
        for c, (dz, dx) in enumerate(CORNERS):
            z0, z1, x0, x1, there = corner_places(dz, dx)
            pa[z0, x0 : x0 + 1, :] = jnp.where(there, dr[c], 0.0)

    everyone("xy", xy, me, hops_xy, lambda to: s2.at[to], r2, a2s, a2r, second_halo)

    block = lax.broadcasted_iota(jnp.int32, (coarse, half * 2), 1) // xy
    for base, deep in ((0, coarse), (4, 8)):
        turned = jnp.concatenate([r2[:, base + e : base + e + 1, :].reshape(xy, wide) for e in range(4)], axis=0).T
        for e in range(4):
            for j in range(2):
                mixed = jnp.zeros((deep, 4 * xy), jnp.float32)
                for b in range(4):
                    at = (4 * j + b) * coarse
                    piece, shift = turned[at : at + deep, :], (b - e) % 4 * xy
                    piece = pltpu.roll(piece, shift, 1) if shift else piece
                    mixed = jnp.where(block[:deep] == b, piece, mixed)
                for twice in range(2):
                    row, count = (2 * e + twice, coarse) if base == 0 else (wide + 2 * e + twice, 2)
                    tm.at[j][pl.ds(row, count, stride=8), :] = mixed[:count]
    cc[...] = dot3(jnp.concatenate([tm[0], tm[1]], axis=1), ty, ((1,), (0,))).reshape(coarse + 2, 8, ny)

    def lift(z, carry):
        fix = cc[z]
        pa[2 * z + 3] = pa[2 * z + 3] + fix
        pa[2 * z + 4] = pa[2 * z + 4] + fix
        return carry

    lax.fori_loop(0, coarse, lift, 0, unroll=2)
    for i, z in ((1, coarse), (2, coarse), (top, coarse + 1), (top + 1, coarse + 1)):
        pa[i] = pa[i] + cc[z]
    sweep(pa, pb, 1)

    def last_sweep(i, carry):
        potv[i - 3] = relax(pb, i)[2:6, :]
        return carry

    part = planes // 4
    leaving = []
    for c in range(4):
        lax.fori_loop(3 + c * part, 3 + (c + 1) * part, last_sweep, 0, unroll=4)
        here = pl.ds(c * part, part)
        leaving.append(pltpu.make_async_copy(potv.at[here], out_hbm.at[here], outs.at[c]))
        leaving[-1].start()
    for copy in leaving:
        copy.wait()


def body(gz, xy, consts, source, potential):
    planes, rows, ny = source.shape
    coarse = planes // 2
    wide, two = coarse * 8, 4 * xy
    f32 = jnp.float32
    vm = lambda *shape: pltpu.VMEM(shape, f32)
    half = lambda *shape: pltpu.VMEM((2, *shape), jnp.bfloat16)
    dma = lambda n: pltpu.SemaphoreType.DMA((n,))
    scratch = [
        vm(planes, rows, ny), vm(planes, rows, ny), half(M * xy, ny), half(2 * xy, two), half(8 * xy, two), vm(M, two),
        vm(planes + 6, 8, ny), vm(planes + 6, 8, ny), vm(planes + 4, 8, ny),
        vm(2, planes, 2, ny), vm(2, planes, 2, ny), vm(2, planes, 1, ny), vm(2, planes + 4, 1, ny),
        vm(2, planes, 2, ny), vm(2, planes, 2, ny),
        vm(2, 3, rows, ny), vm(2, 2, rows, ny), vm(4, 4, ny), vm(4, 4, ny),
        vm(2, planes, 2, ny), vm(2, planes, 2, ny), vm(2, 2, 8, ny), vm(4, 1, ny), vm(4, 1, ny),
        vm(coarse, 8, ny), vm(xy, 2, wide), vm(xy, 2, wide), vm(coarse, M, two), vm(coarse, M, two),
        vm(M, two), vm(gz, M, two), vm(wide, two), vm(xy, 8, wide), vm(xy, 8, wide),
        vm(2, wide + 16, 4 * xy), vm(coarse + 2, 8, ny),
        dma(6), dma(14), dma(14), dma(8), dma(8), dma(1), dma(1), dma(1), dma(1), dma(1), dma(1), dma(4),
        pltpu.SemaphoreType.REGULAR((4,)), pltpu.SemaphoreType.REGULAR((4,)),
    ]
    hbm = pl.BlockSpec(memory_space=pl.ANY)
    return pl.pallas_call(
        functools.partial(kernel, gz, xy),
        out_shape=jax.ShapeDtypeStruct(source.shape, f32),
        in_specs=[pl.BlockSpec(memory_space=pltpu.HBM)] * 6,
        out_specs=hbm,
        scratch_shapes=scratch,
        compiler_params=pltpu.CompilerParams(vmem_limit_bytes=24 * 1024 * 1024, collective_id=0, has_side_effects=True),
        name="vcycle",
    )(*[pltpu.with_memory_space_constraint(a, pltpu.HBM) for a in (source, potential, *map(jnp.asarray, consts))])


def solution(mesh):
    gz, xy = mesh.shape["gz"], mesh.shape["xy"]
    consts = tables(xy)
    placed = (P("gz", "xy", None), P("gz", "xy", None))
    return jax.shard_map(
        functools.partial(body, gz, xy, consts), mesh=mesh, in_specs=placed,
        out_specs=P("gz", "xy", None), check_vma=False,
    )
```

```python
import functools
import math

import jax
import jax.numpy as jnp
import ml_dtypes
import numpy as np
from jax import lax
from jax.experimental import pallas as pl
from jax.experimental.pallas import tpu as pltpu
from jax.sharding import PartitionSpec as P

SCREEN = 64
OMEGA = 0.8
KAPPA = 1.0 / (SCREEN * SCREEN)
CW = 6.0 + KAPPA
M = 8
CORNERS = ((-1, -1), (-1, 1), (1, -1), (1, 1))


def sine(count):
    idx = np.arange(1, count + 1, dtype=np.int64)
    turns = idx[:, None] * idx[None, :] % (2 * (count + 1))
    return math.sqrt(2.0 / (count + 1)) * np.sin(math.pi / (count + 1) * turns)


def eigen(count):
    return 2.0 - 2.0 * np.cos(math.pi / (count + 1) * np.arange(1, count + 1))


def two_parts(table):
    coarse = table.astype(ml_dtypes.bfloat16)
    return np.stack([coarse, (table - coarse.astype(np.float64)).astype(ml_dtypes.bfloat16)])


def dot3(value, table, dims):
    coarse = value.astype(jnp.bfloat16)
    fine = (value - coarse.astype(jnp.float32)).astype(jnp.bfloat16)
    dot = lambda a, b: lax.dot_general(a, b, (dims, ((), ())), preferred_element_type=jnp.float32)
    return dot(coarse, table[0]) + dot(fine, table[0]) + dot(coarse, table[1])


def dot3_table_first(table, value, dims):
    coarse = value.astype(jnp.bfloat16)
    fine = (value - coarse.astype(jnp.float32)).astype(jnp.bfloat16)
    dot = lambda a, b: lax.dot_general(a, b, (dims, ((), ())), preferred_element_type=jnp.float32)
    return dot(table[0], coarse) + dot(table[0], fine) + dot(table[1], coarse)


def tables(groups):
    nx, ny = 2 * groups, M * groups
    sx, sy = sine(nx), sine(ny)
    ty = np.repeat(sy, 2, axis=1)
    order = np.concatenate([np.arange(0, nx, 2), np.arange(1, nx, 2)])
    fx = 0.5 * np.concatenate([sx[order], sx[order]], axis=1)
    bx = np.zeros((groups, 8, 2 * nx))
    for d in range(groups):
        for e in range(4):
            x = 2 * d - 1 + e
            if 0 <= x < nx:
                bx[d, e, :nx] = sx[x]
                bx[d, 4 + e, nx:] = sx[x]
    diag = 2.0 + eigen(nx)[None, None, :] + eigen(ny).reshape(M, groups).T[:, :, None] + 4.0 * KAPPA
    theta = np.arccosh(0.5 * diag)
    theta = np.concatenate([theta, theta], axis=2)
    return two_parts(ty), two_parts(fx), two_parts(bx.reshape(groups * 8, 2 * nx)), theta.astype(np.float32)


def kernel(
    gz, xy, src_hbm, pot_hbm, ty_hbm, fx_hbm, bx_hbm, th_hbm, out_hbm,
    potv, srcv, ty, fx, bx, th, pa, pb, sv,
    xps, xpr, xts, xtr, xss, xsr, zpr, zsr, cs, cr,
    xqs, xqr, zqr, ds, dr,
    rs, s1, r1, fz, wz, ztile, zr, vz, s2, r2, tm, cc,
    ld, e1s, e1r, e2s, e2r, a1s, a1r, gs, gr, a2s, a2r, outs, known_x, known_z,
):
    q, me = lax.axis_index("gz"), lax.axis_index("xy")
    planes, rows, ny = potv.shape
    half = 2 * xy
    top = planes + 3

    loads = [
        pltpu.make_async_copy(pot_hbm, potv, ld.at[0]),
        pltpu.make_async_copy(src_hbm, srcv, ld.at[1]),
        pltpu.make_async_copy(ty_hbm, ty, ld.at[2]),
        pltpu.make_async_copy(fx_hbm, fx, ld.at[3]),
        pltpu.make_async_copy(bx_hbm, bx, ld.at[4]),
        pltpu.make_async_copy(th_hbm.at[me], th, ld.at[5]),
    ]
    def shifted(dz, dx):
        where = {}
        if dz:
            where["gz"] = lax.rem(q + dz + gz, gz)
        if dx:
            where["xy"] = lax.rem(me + dx + xy, xy)
        return where

    def tell(sem, where):
        pl.semaphore_signal(sem, inc=1, device_id=where, device_id_type=pl.DeviceIdType.MESH)

    barrier = pltpu.get_barrier_semaphore()
    for dz, dx in CORNERS + ((-1, 0), (1, 0), (0, -1), (0, 1)):
        tell(barrier, shifted(dz, dx))
    loads[0].start()
    loads[1].start()

    for side in range(2):
        xtr[side, 0:2] = jnp.zeros((2, 1, ny), jnp.float32)
        xtr[side, planes + 2 : planes + 4] = jnp.zeros((2, 1, ny), jnp.float32)
    loads[0].wait()
    xps[0] = potv[:, 0:2, :]
    xps[1] = potv[:, 2:4, :]
    xts[0] = potv[:, 2:3, :]
    xts[1] = potv[:, 1:2, :]
    pl.semaphore_wait(barrier, 8)

    def round_of(level):
        for axis, size, dim, known in (("xy", xy, 1, known_x), ("gz", gz, 0, known_z)):
            reach = 2**level
            if level and reach // 2 < size // 2:
                pl.semaphore_wait(known.at[level - 1], 2)
            if reach < size // 2:
                for way in (-reach, reach):
                    tell(known.at[level], shifted(way, 0) if dim == 0 else shifted(0, way))

    class Exchange:
        def __init__(self, send, recv):
            self.send, self.recv, self.copies = send, recv, []

        def add(self, src, dst, dz, dx):
            slot = len(self.copies)
            copy = remote(src, dst, self.send.at[slot], self.recv.at[slot], shifted(dz, dx))
            self.copies.append((copy, exists(dz, dx), exists(-dz, -dx)))

        def start(self, slot):
            copy, there, unused = self.copies[slot]
            pl.when(there)(copy.start)

        def wait(self):
            for copy, there, back in self.copies:
                pl.when(back)(copy.wait_recv)
                pl.when(there)(copy.wait_send)

    def exists(dz, dx):
        there = None
        for step, mine, size in ((dz, q, gz), (dx, me, xy)):
            if step:
                ok = mine > 0 if step < 0 else mine < size - 1
                there = ok if there is None else jnp.logical_and(there, ok)
        return there

    def remote(src, dst, send, recv, where):
        return pltpu.make_async_remote_copy(
            src_ref=src, dst_ref=dst, send_sem=send, recv_sem=recv,
            device_id=where, device_id_type=pl.DeviceIdType.MESH,
        )

    first = Exchange(e1s, e1r)
    for side, step in ((0, -1), (1, 1)):
        first.add(xps.at[side], xpr.at[side], 0, step)
        first.add(xts.at[side], xtr.at[side, pl.ds(2, planes)], 0, step)
        first.add(xss.at[side], xsr.at[side], 0, step)
        first.add(potv.at[pl.ds(0 if step < 0 else planes - 3, 3)], zpr.at[side], step, 0)
        first.add(srcv.at[pl.ds(0 if step < 0 else planes - 2, 2)], zsr.at[side], step, 0)
    for c, (dz, dx) in enumerate(CORNERS):
        first.add(cs.at[c], cr.at[c], dz, dx)
    for slot in (0, 5, 1, 6, 3, 8):
        first.start(slot)
    round_of(0)
    loads[1].wait()
    xss[0] = srcv[:, 0:2, :]
    xss[1] = srcv[:, 2:4, :]
    for c, (dz, dx) in enumerate(CORNERS):
        z0, z1 = (0, 1) if dz < 0 else (planes - 1, planes - 2)
        x0, x1 = (0, 1) if dx < 0 else (rows - 1, rows - 2)
        cs[c, 0:1] = potv[z0, x0 : x0 + 1, :]
        cs[c, 1:2] = potv[z0, x1 : x1 + 1, :]
        cs[c, 2:3] = potv[z1, x0 : x0 + 1, :]
        cs[c, 3:4] = srcv[z0, x0 : x0 + 1, :]
    for slot in (2, 7, 4, 9, 10, 11, 12, 13):
        first.start(slot)
    for copy in loads[2:]:
        copy.start()

    pa[...] = jnp.zeros_like(pa)
    sv[...] = jnp.zeros_like(sv)
    pa[3:top, 2:6, :] = potv[...]
    sv[2 : planes + 2, 2:6, :] = srcv[...]
    sub = lax.broadcasted_iota(jnp.int32, (8, ny), 0)
    lane = lax.broadcasted_iota(jnp.int32, (8, ny), 1)
    inside = jnp.logical_and(
        jnp.logical_or(sub >= 2, me > 0), jnp.logical_or(sub < 6, me < xy - 1)
    )
    has_low, has_high, has_near, has_far = q > 0, q < gz - 1, me > 0, me < xy - 1

    def corner_places(dz, dx):
        z0, z1 = (top, top + 1) if dz < 0 else (2, 1)
        x0, x1 = (6, 7) if dx < 0 else (1, 0)
        return z0, z1, x0, x1, exists(-dz, -dx)

    round_of(1)
    round_of(2)
    first.wait()
    round_of(3)
    pa[3:top, 0:2, :] = jnp.where(has_near, xpr[1], 0.0)
    pa[3:top, 6:8, :] = jnp.where(has_far, xpr[0], 0.0)
    pa[0:3, 2:6, :] = jnp.where(has_low, zpr[1], 0.0)
    pa[top : top + 3, 2:6, :] = jnp.where(has_high, zpr[0], 0.0)
    sv[2 : planes + 2, 0:2, :] = jnp.where(has_near, xsr[1], 0.0)
    sv[2 : planes + 2, 6:8, :] = jnp.where(has_far, xsr[0], 0.0)
    sv[0:2, 2:6, :] = jnp.where(has_low, zsr[1], 0.0)
    sv[planes + 2 : planes + 4, 2:6, :] = jnp.where(has_high, zsr[0], 0.0)
    for c, (dz, dx) in enumerate(CORNERS):
        z0, z1, x0, x1, there = corner_places(dz, dx)
        corner = jnp.where(there, cr[c], 0.0)
        pa[z0, x0 : x0 + 1, :] = corner[0:1]
        pa[z0, x1 : x1 + 1, :] = corner[1:2]
        pa[z1, x0 : x0 + 1, :] = corner[2:3]
        sv[z0 - 1, x0 : x0 + 1, :] = corner[3:4]

    def row_sum(v):
        before = jnp.where(lane == 0, 0.0, pltpu.roll(v, 1, 1))
        return before + jnp.where(lane == ny - 1, 0.0, pltpu.roll(v, ny - 1, 1))

    def flat_sum(v):
        return pltpu.roll(v, 1, 0) + pltpu.roll(v, 7, 0) + row_sum(v)

    def neighbours(ref, i, ends=None):
        v = ref[i]
        total = ref[i - 1] + ref[i + 1]
        back, forth = pltpu.roll(v, 1, 0), pltpu.roll(v, 7, 0)
        if ends is not None:
            back, forth = jnp.where(sub == 0, ends[0], back), jnp.where(sub == 7, ends[1], forth)
        return v, total + back + forth + row_sum(v)

    def relax(ref, i, ends=None):
        v, total = neighbours(ref, i, ends)
        return (1.0 - OMEGA) * v + (OMEGA / CW) * (sv[i - 1] + total)

    def sweep(src, dst, ring, ended=False):
        def step(i, carry):
            ends = None
            if ended:
                ends = [jnp.where(there, xtr[side, i - 1], 0.0) for there, side in ((has_near, 1), (has_far, 0))]
            dst[i] = jnp.where(inside, relax(src, i, ends), 0.0)
            return carry

        if ring == 2:
            lax.fori_loop(1, top + 2, step, 0, unroll=4)
        else:
            lax.fori_loop(3, top, step, 0, unroll=4)
            step(2, 0)
            step(top, 0)
        for i in range(ring):
            dst[2 - i] = jnp.where(has_low, dst[2 - i], 0.0)
            dst[top + i] = jnp.where(has_high, dst[top + i], 0.0)

    sweep(pa, pb, 2, True)
    sweep(pb, pa, 1)
    round_of(4)

    xqs[0] = pa[3:top, 2:4, :]
    xqs[1] = pa[3:top, 4:6, :]
    for c, (dz, dx) in enumerate(CORNERS):
        z, x = 3 if dz < 0 else top - 1, 2 if dx < 0 else 5
        ds[c] = pa[z, x : x + 1, :]
    second = Exchange(e2s, e2r)
    for side, step in ((0, -1), (1, 1)):
        second.add(xqs.at[side], xqr.at[side], 0, step)
        second.add(pa.at[pl.ds(3 if step < 0 else top - 2, 2)], zqr.at[side], step, 0)
    for c, (dz, dx) in enumerate(CORNERS):
        second.add(ds.at[c], dr.at[c], dz, dx)
    for slot in (1, 3, 4, 5, 6, 7):
        second.start(slot)

    def residual(i):
        v, total = neighbours(pa, i)
        return sv[i - 1] - CW * v + total

    def coarsen(z, carry):
        rs[z] = residual(2 * z + 3) + residual(2 * z + 4)
        return carry

    coarse = planes // 2
    lax.fori_loop(0, coarse, coarsen, 0, unroll=2)
    for copy in loads[2:]:
        copy.wait()
    wide = coarse * 8
    spec = dot3_table_first(ty, rs[...].reshape(wide, ny), ((1,), (1,)))
    spec = spec + pltpu.roll(spec, wide - 1, 1)
    slot = lax.broadcasted_iota(jnp.int32, (xy, wide), 1) % 8
    for xx in range(2):
        packed = jnp.zeros((xy, wide), jnp.float32)
        for m in range(M):
            piece = spec[m * xy : (m + 1) * xy, :]
            shift = (m - 2 - 2 * xx) % wide
            piece = pltpu.roll(piece, shift, 1) if shift else piece
            packed = jnp.where(slot == m, piece, packed)
        s1[:, xx : xx + 1, :] = packed.reshape(xy, 1, wide)

    def everyone(axis, size, mine, far, src_of, dst, send, recv, meanwhile=None):
        for i in sorted(range(1, size), key=far, reverse=True):
            to = lax.rem(mine + i, size)
            remote(src_of(to), dst.at[mine], send.at[0], recv.at[0], {axis: to}).start()
        dst[mine] = src_of(mine)[...]
        if meanwhile is not None:
            meanwhile()
        rest = dst.at[pl.ds(0, size - 1)]
        done = remote(rest, rest, send.at[0], recv.at[0], {axis: lax.rem(mine + 1, size)})
        done.wait_recv()
        done.wait_send()

    def hops_xy(i):
        return min(i // 8, 4 - i // 8) + min(i % 8 // 2, 4 - i % 8 // 2)

    def hops_z(i):
        return min(i, gz - i)

    everyone("xy", xy, me, hops_xy, lambda to: s1.at[to], r1, a1s, a1r)
    second.start(0)
    second.start(2)
    gathered = jnp.concatenate([r1[:, 0:1, :].reshape(xy, wide), r1[:, 1:2, :].reshape(xy, wide)], axis=0)
    fz[...] = dot3(gathered.T, fx, ((1,), (0,))).reshape(coarse, M, 2 * half)

    up = lax.broadcasted_iota(jnp.int32, (M, 2 * half), 1) < half
    theta = th[...]
    decay = jnp.exp(-theta)
    state = jnp.zeros((M, 2 * half), jnp.float32)
    for t in range(coarse):
        state = decay * state + jnp.where(up, fz[t], fz[coarse - 1 - t])
        wz[t] = state
    ztile[...] = state
    everyone("gz", gz, q, hops_z, lambda to: ztile, zr, gs, gr)
    slab = jnp.exp(-float(coarse) * theta)
    total = jnp.zeros((M, 2 * half), jnp.float32)
    inflow = jnp.zeros((M, 2 * half), jnp.float32)
    steps_in = jnp.where(up, q, gz - 1 - q)
    for t in range(gz):
        inflow = jnp.where(steps_in == t, total, inflow)
        total = slab * total + jnp.where(up, zr[t], zr[gz - 1 - t])
    span = float(coarse * gz + 1)
    image = pltpu.roll(total, half, 1) - jnp.exp(-span * theta) * total
    image = image * jnp.exp(-theta * (float(coarse) * steps_in.astype(jnp.float32) + 1.0))
    inflow = inflow - image / (1.0 - jnp.exp(-2.0 * span * theta))
    scale = 1.0 / (jnp.exp(theta) - decay)
    power = decay
    for t in range(coarse):
        wz[t] = wz[t] + power * inflow
        power = power * decay
    last = decay * wz[coarse - 1]
    beyond = scale * (last + pltpu.roll(inflow, half, 1))
    above, below = jnp.where(has_high, beyond, 0.0), jnp.where(has_low, beyond, 0.0)
    above = pltpu.roll(above, half, 1)
    for z in range(coarse):
        value = scale * (wz[z] + pltpu.roll(wz[coarse - 1 - z], half, 1) - fz[z])
        ring = below if z == 0 else above if z == 1 else 0.0
        vz[pl.ds(z, M, stride=coarse), :] = jnp.where(up, value, ring)
    s2[...] = dot3_table_first(bx, vz[...], ((1,), (1,))).reshape(xy, 8, wide)
    def second_halo():
        second.wait()
        pa[3:top, 0:2, :] = jnp.where(has_near, xqr[1], 0.0)
        pa[3:top, 6:8, :] = jnp.where(has_far, xqr[0], 0.0)
        pa[1:3, 2:6, :] = jnp.where(has_low, zqr[1, :, 2:6, :], 0.0)
        pa[top : top + 2, 2:6, :] = jnp.where(has_high, zqr[0, :, 2:6, :], 0.0)
        for c, (dz, dx) in enumerate(CORNERS):
            z0, z1, x0, x1, there = corner_places(dz, dx)
            pa[z0, x0 : x0 + 1, :] = jnp.where(there, dr[c], 0.0)

        sweep(pa, pb, 1)

        def base_sweep(i, carry):
            pa[i] = relax(pb, i)
            return carry

        lax.fori_loop(3, top, base_sweep, 0, unroll=4)

    everyone("xy", xy, me, hops_xy, lambda to: s2.at[to], r2, a2s, a2r, second_halo)

    block = lax.broadcasted_iota(jnp.int32, (coarse, half * 2), 1) // xy
    for base, deep in ((0, coarse), (4, 8)):
        turned = jnp.concatenate([r2[:, base + e : base + e + 1, :].reshape(xy, wide) for e in range(4)], axis=0).T
        for e in range(4):
            for j in range(2):
                mixed = jnp.zeros((deep, 4 * xy), jnp.float32)
                for b in range(4):
                    at = (4 * j + b) * coarse
                    piece, shift = turned[at : at + deep, :], (b - e) % 4 * xy
                    piece = pltpu.roll(piece, shift, 1) if shift else piece
                    mixed = jnp.where(block[:deep] == b, piece, mixed)
                for twice in range(2):
                    row, count = (2 * e + twice, coarse) if base == 0 else (wide + 2 * e + twice, 2)
                    tm.at[j][pl.ds(row, count, stride=8), :] = mixed[:count]
    fixes = dot3(jnp.concatenate([tm[0], tm[1]], axis=1), ty, ((1,), (0,))).reshape(coarse + 2, 8, ny)
    cc[1 : coarse + 1] = fixes[:coarse]
    cc[0] = fixes[coarse]
    cc[coarse + 1] = fixes[coarse + 1]

    gain = OMEGA / CW

    def shared(z):
        v = cc[z]
        total = v + flat_sum(v)
        return (1.0 - OMEGA) * v + gain * total

    def lifted_sweep(z, carry):
        common = shared(z)
        pb[2 * z + 1] = jnp.where(inside, common + gain * cc[z - 1], 0.0)
        pb[2 * z + 2] = jnp.where(inside, common + gain * cc[z + 1], 0.0)
        return carry

    lax.fori_loop(1, coarse + 1, lifted_sweep, 0, unroll=2)
    pb[2] = jnp.where(jnp.logical_and(inside, has_low), shared(0) + gain * cc[1], 0.0)
    pb[top] = jnp.where(jnp.logical_and(inside, has_high), shared(coarse + 1) + gain * cc[coarse], 0.0)

    def last_sweep(i, carry):
        v, total = neighbours(pb, i)
        potv[i - 3] = (pa[i] + (1.0 - OMEGA) * v + gain * total)[2:6, :]
        return carry

    part = planes // 4
    leaving = []
    for c in range(4):
        lax.fori_loop(3 + c * part, 3 + (c + 1) * part, last_sweep, 0, unroll=4)
        here = pl.ds(c * part, part)
        leaving.append(pltpu.make_async_copy(potv.at[here], out_hbm.at[here], outs.at[c]))
        leaving[-1].start()
    for copy in leaving:
        copy.wait()


def body(gz, xy, consts, source, potential):
    planes, rows, ny = source.shape
    coarse = planes // 2
    wide, two = coarse * 8, 4 * xy
    f32 = jnp.float32
    vm = lambda *shape: pltpu.VMEM(shape, f32)
    half = lambda *shape: pltpu.VMEM((2, *shape), jnp.bfloat16)
    dma = lambda n: pltpu.SemaphoreType.DMA((n,))
    scratch = [
        vm(planes, rows, ny), vm(planes, rows, ny), half(M * xy, ny), half(2 * xy, two), half(8 * xy, two), vm(M, two),
        vm(planes + 6, 8, ny), vm(planes + 6, 8, ny), vm(planes + 4, 8, ny),
        vm(2, planes, 2, ny), vm(2, planes, 2, ny), vm(2, planes, 1, ny), vm(2, planes + 4, 1, ny),
        vm(2, planes, 2, ny), vm(2, planes, 2, ny),
        vm(2, 3, rows, ny), vm(2, 2, rows, ny), vm(4, 4, ny), vm(4, 4, ny),
        vm(2, planes, 2, ny), vm(2, planes, 2, ny), vm(2, 2, 8, ny), vm(4, 1, ny), vm(4, 1, ny),
        vm(coarse, 8, ny), vm(xy, 2, wide), vm(xy, 2, wide), vm(coarse, M, two), vm(coarse, M, two),
        vm(M, two), vm(gz, M, two), vm(wide, two), vm(xy, 8, wide), vm(xy, 8, wide),
        vm(2, wide + 16, 4 * xy), vm(coarse + 2, 8, ny),
        dma(6), dma(14), dma(14), dma(8), dma(8), dma(1), dma(1), dma(1), dma(1), dma(1), dma(1), dma(4),
        pltpu.SemaphoreType.REGULAR((4,)), pltpu.SemaphoreType.REGULAR((4,)),
    ]
    hbm = pl.BlockSpec(memory_space=pl.ANY)
    return pl.pallas_call(
        functools.partial(kernel, gz, xy),
        out_shape=jax.ShapeDtypeStruct(source.shape, f32),
        in_specs=[pl.BlockSpec(memory_space=pltpu.HBM)] * 6,
        out_specs=hbm,
        scratch_shapes=scratch,
        compiler_params=pltpu.CompilerParams(vmem_limit_bytes=24 * 1024 * 1024, collective_id=0, has_side_effects=True),
        name="vcycle",
    )(*[pltpu.with_memory_space_constraint(a, pltpu.HBM) for a in (source, potential, *map(jnp.asarray, consts))])


def solution(mesh):
    gz, xy = mesh.shape["gz"], mesh.shape["xy"]
    consts = tables(xy)
    placed = (P("gz", "xy", None), P("gz", "xy", None))
    return jax.shard_map(
        functools.partial(body, gz, xy, consts), mesh=mesh, in_specs=placed,
        out_specs=P("gz", "xy", None), check_vma=False,
    )
```

```python
import functools
import math

import jax
import jax.numpy as jnp
import ml_dtypes
import numpy as np
from jax import lax
from jax.experimental import pallas as pl
from jax.experimental.pallas import tpu as pltpu
from jax.sharding import PartitionSpec as P

SCREEN = 64
OMEGA = 0.8
KAPPA = 1.0 / (SCREEN * SCREEN)
CW = 6.0 + KAPPA
M = 8
CORNERS = ((-1, -1), (-1, 1), (1, -1), (1, 1))


def sine(count):
    idx = np.arange(1, count + 1, dtype=np.int64)
    turns = idx[:, None] * idx[None, :] % (2 * (count + 1))
    return math.sqrt(2.0 / (count + 1)) * np.sin(math.pi / (count + 1) * turns)


def eigen(count):
    return 2.0 - 2.0 * np.cos(math.pi / (count + 1) * np.arange(1, count + 1))


def two_parts(table):
    coarse = table.astype(ml_dtypes.bfloat16)
    return np.stack([coarse, (table - coarse.astype(np.float64)).astype(ml_dtypes.bfloat16)])


def dot3(value, table, dims):
    coarse = value.astype(jnp.bfloat16)
    fine = (value - coarse.astype(jnp.float32)).astype(jnp.bfloat16)
    dot = lambda a, b: lax.dot_general(a, b, (dims, ((), ())), preferred_element_type=jnp.float32)
    return dot(coarse, table[0]) + dot(fine, table[0]) + dot(coarse, table[1])


def dot3_table_first(table, value, dims):
    coarse = value.astype(jnp.bfloat16)
    fine = (value - coarse.astype(jnp.float32)).astype(jnp.bfloat16)
    dot = lambda a, b: lax.dot_general(a, b, (dims, ((), ())), preferred_element_type=jnp.float32)
    return dot(table[0], coarse) + dot(table[0], fine) + dot(table[1], coarse)


def tables(groups):
    nx, ny = 2 * groups, M * groups
    sx, sy = sine(nx), sine(ny)
    ty = np.repeat(sy, 2, axis=1)
    order = np.concatenate([np.arange(0, nx, 2), np.arange(1, nx, 2)])
    fx = 0.5 * np.concatenate([sx[order], sx[order]], axis=1)
    bx = np.zeros((groups, 8, 2 * nx))
    for d in range(groups):
        for e in range(4):
            x = 2 * d - 1 + e
            if 0 <= x < nx:
                bx[d, e, :nx] = sx[x]
                bx[d, 4 + e, nx:] = sx[x]
    diag = 2.0 + eigen(nx)[None, None, :] + eigen(ny).reshape(M, groups).T[:, :, None] + 4.0 * KAPPA
    theta = np.arccosh(0.5 * diag)
    theta = np.concatenate([theta, theta], axis=2)
    return two_parts(ty), two_parts(fx), two_parts(bx.reshape(groups * 8, 2 * nx)), theta.astype(np.float32)


def kernel(
    gz, xy, src_hbm, pot_hbm, ty_hbm, fx_hbm, bx_hbm, th_hbm, out_hbm,
    potv, srcv, ty, fx, bx, th, pa, pb, sv,
    xps, xpr, xts, xtr, xss, xsr, zpr, zsr, cs, cr,
    xqs, xqr, zqr, ds, dr,
    rs, s1, r1, fz, wz, ztile, zr, vz, s2, r2, tm, cc,
    ld, e1s, e1r, e2s, e2r, a1s, a1r, gs, gr, a2s, a2r, outs, known_x, known_z,
):
    q, me = lax.axis_index("gz"), lax.axis_index("xy")
    planes, rows, ny = potv.shape
    half = 2 * xy
    top = planes + 3

    loads = [
        pltpu.make_async_copy(pot_hbm, potv, ld.at[0]),
        pltpu.make_async_copy(src_hbm, srcv, ld.at[1]),
        pltpu.make_async_copy(ty_hbm, ty, ld.at[2]),
        pltpu.make_async_copy(fx_hbm, fx, ld.at[3]),
        pltpu.make_async_copy(bx_hbm, bx, ld.at[4]),
        pltpu.make_async_copy(th_hbm.at[me], th, ld.at[5]),
    ]
    def shifted(dz, dx):
        where = {}
        if dz:
            where["gz"] = lax.rem(q + dz + gz, gz)
        if dx:
            where["xy"] = lax.rem(me + dx + xy, xy)
        return where

    def tell(sem, where):
        pl.semaphore_signal(sem, inc=1, device_id=where, device_id_type=pl.DeviceIdType.MESH)

    barrier = pltpu.get_barrier_semaphore()
    for dz, dx in CORNERS + ((-1, 0), (1, 0), (0, -1), (0, 1)):
        tell(barrier, shifted(dz, dx))
    loads[0].start()
    loads[1].start()

    for side in range(2):
        xtr[side, 0:2] = jnp.zeros((2, 1, ny), jnp.float32)
        xtr[side, planes + 2 : planes + 4] = jnp.zeros((2, 1, ny), jnp.float32)
    loads[0].wait()
    xps[0] = potv[:, 0:2, :]
    xps[1] = potv[:, 2:4, :]
    xts[0] = potv[:, 2:3, :]
    xts[1] = potv[:, 1:2, :]
    pl.semaphore_wait(barrier, 8)

    def round_of(level):
        for axis, size, dim, known in (("xy", xy, 1, known_x), ("gz", gz, 0, known_z)):
            reach = 2**level
            if level and reach // 2 < size // 2:
                pl.semaphore_wait(known.at[level - 1], 2)
            if reach < size // 2:
                for way in (-reach, reach):
                    tell(known.at[level], shifted(way, 0) if dim == 0 else shifted(0, way))

    class Exchange:
        def __init__(self, send, recv):
            self.send, self.recv, self.copies = send, recv, []

        def add(self, src, dst, dz, dx):
            slot = len(self.copies)
            copy = remote(src, dst, self.send.at[slot], self.recv.at[slot], shifted(dz, dx))
            self.copies.append((copy, exists(dz, dx), exists(-dz, -dx)))

        def start(self, slot):
            copy, there, unused = self.copies[slot]
            pl.when(there)(copy.start)

        def wait(self):
            for copy, there, back in self.copies:
                pl.when(back)(copy.wait_recv)
                pl.when(there)(copy.wait_send)

    def exists(dz, dx):
        there = None
        for step, mine, size in ((dz, q, gz), (dx, me, xy)):
            if step:
                ok = mine > 0 if step < 0 else mine < size - 1
                there = ok if there is None else jnp.logical_and(there, ok)
        return there

    def remote(src, dst, send, recv, where):
        return pltpu.make_async_remote_copy(
            src_ref=src, dst_ref=dst, send_sem=send, recv_sem=recv,
            device_id=where, device_id_type=pl.DeviceIdType.MESH,
        )

    first = Exchange(e1s, e1r)
    for side, step in ((0, -1), (1, 1)):
        first.add(xps.at[side], xpr.at[side], 0, step)
        first.add(xts.at[side], xtr.at[side, pl.ds(2, planes)], 0, step)
        first.add(xss.at[side], xsr.at[side], 0, step)
        first.add(potv.at[pl.ds(0 if step < 0 else planes - 3, 3)], zpr.at[side], step, 0)
        first.add(srcv.at[pl.ds(0 if step < 0 else planes - 2, 2)], zsr.at[side], step, 0)
    for c, (dz, dx) in enumerate(CORNERS):
        first.add(cs.at[c], cr.at[c], dz, dx)
    for slot in (0, 5, 1, 6, 3, 8):
        first.start(slot)
    round_of(0)
    loads[1].wait()
    xss[0] = srcv[:, 0:2, :]
    xss[1] = srcv[:, 2:4, :]
    for c, (dz, dx) in enumerate(CORNERS):
        z0, z1 = (0, 1) if dz < 0 else (planes - 1, planes - 2)
        x0, x1 = (0, 1) if dx < 0 else (rows - 1, rows - 2)
        cs[c, 0:1] = potv[z0, x0 : x0 + 1, :]
        cs[c, 1:2] = potv[z0, x1 : x1 + 1, :]
        cs[c, 2:3] = potv[z1, x0 : x0 + 1, :]
        cs[c, 3:4] = srcv[z0, x0 : x0 + 1, :]
    for slot in (2, 7, 4, 9, 10, 11, 12, 13):
        first.start(slot)
    for copy in loads[2:]:
        copy.start()

    pa[...] = jnp.zeros_like(pa)
    sv[...] = jnp.zeros_like(sv)
    pa[3:top, 2:6, :] = potv[...]
    sv[2 : planes + 2, 2:6, :] = srcv[...]
    sub = lax.broadcasted_iota(jnp.int32, (8, ny), 0)
    lane = lax.broadcasted_iota(jnp.int32, (8, ny), 1)
    inside = jnp.logical_and(
        jnp.logical_or(sub >= 2, me > 0), jnp.logical_or(sub < 6, me < xy - 1)
    )
    has_low, has_high, has_near, has_far = q > 0, q < gz - 1, me > 0, me < xy - 1

    def corner_places(dz, dx):
        z0, z1 = (top, top + 1) if dz < 0 else (2, 1)
        x0, x1 = (6, 7) if dx < 0 else (1, 0)
        return z0, z1, x0, x1, exists(-dz, -dx)

    round_of(1)
    round_of(2)
    first.wait()
    pa[3:top, 0:2, :] = jnp.where(has_near, xpr[1], 0.0)
    pa[3:top, 6:8, :] = jnp.where(has_far, xpr[0], 0.0)
    pa[0:3, 2:6, :] = jnp.where(has_low, zpr[1], 0.0)
    pa[top : top + 3, 2:6, :] = jnp.where(has_high, zpr[0], 0.0)
    sv[2 : planes + 2, 0:2, :] = jnp.where(has_near, xsr[1], 0.0)
    sv[2 : planes + 2, 6:8, :] = jnp.where(has_far, xsr[0], 0.0)
    sv[0:2, 2:6, :] = jnp.where(has_low, zsr[1], 0.0)
    sv[planes + 2 : planes + 4, 2:6, :] = jnp.where(has_high, zsr[0], 0.0)
    for c, (dz, dx) in enumerate(CORNERS):
        z0, z1, x0, x1, there = corner_places(dz, dx)
        corner = jnp.where(there, cr[c], 0.0)
        pa[z0, x0 : x0 + 1, :] = corner[0:1]
        pa[z0, x1 : x1 + 1, :] = corner[1:2]
        pa[z1, x0 : x0 + 1, :] = corner[2:3]
        sv[z0 - 1, x0 : x0 + 1, :] = corner[3:4]

    def row_sum(v):
        before = jnp.where(lane == 0, 0.0, pltpu.roll(v, 1, 1))
        return before + jnp.where(lane == ny - 1, 0.0, pltpu.roll(v, ny - 1, 1))

    def flat_sum(v):
        return pltpu.roll(v, 1, 0) + pltpu.roll(v, 7, 0) + row_sum(v)

    def neighbours(ref, i, ends=None):
        v = ref[i]
        total = ref[i - 1] + ref[i + 1]
        back, forth = pltpu.roll(v, 1, 0), pltpu.roll(v, 7, 0)
        if ends is not None:
            back, forth = jnp.where(sub == 0, ends[0], back), jnp.where(sub == 7, ends[1], forth)
        return v, total + back + forth + row_sum(v)

    def relax(ref, i, ends=None):
        v, total = neighbours(ref, i, ends)
        return (1.0 - OMEGA) * v + (OMEGA / CW) * (sv[i - 1] + total)

    def sweep(src, dst, ring, ended=False):
        def step(i, carry):
            ends = None
            if ended:
                ends = [jnp.where(there, xtr[side, i - 1], 0.0) for there, side in ((has_near, 1), (has_far, 0))]
            dst[i] = jnp.where(inside, relax(src, i, ends), 0.0)
            return carry

        if ring == 2:
            lax.fori_loop(1, top + 2, step, 0, unroll=4)
        else:
            lax.fori_loop(3, top, step, 0, unroll=4)
            step(2, 0)
            step(top, 0)
        for i in range(ring):
            dst[2 - i] = jnp.where(has_low, dst[2 - i], 0.0)
            dst[top + i] = jnp.where(has_high, dst[top + i], 0.0)

    sweep(pa, pb, 2, True)
    round_of(3)
    sweep(pb, pa, 1)

    xqs[0] = pa[3:top, 2:4, :]
    xqs[1] = pa[3:top, 4:6, :]
    for c, (dz, dx) in enumerate(CORNERS):
        z, x = 3 if dz < 0 else top - 1, 2 if dx < 0 else 5
        ds[c] = pa[z, x : x + 1, :]
    second = Exchange(e2s, e2r)
    for side, step in ((0, -1), (1, 1)):
        second.add(xqs.at[side], xqr.at[side], 0, step)
        second.add(pa.at[pl.ds(3 if step < 0 else top - 2, 2)], zqr.at[side], step, 0)
    for c, (dz, dx) in enumerate(CORNERS):
        second.add(ds.at[c], dr.at[c], dz, dx)
    for slot in (1, 3, 4, 5, 6, 7):
        second.start(slot)

    def residual(i):
        v, total = neighbours(pa, i)
        return sv[i - 1] - CW * v + total

    def coarsen(z, carry):
        rs[z] = residual(2 * z + 3) + residual(2 * z + 4)
        return carry

    coarse = planes // 2
    lax.fori_loop(0, coarse, coarsen, 0, unroll=2)
    for copy in loads[2:]:
        copy.wait()
    wide = coarse * 8
    spec = dot3_table_first(ty, rs[...].reshape(wide, ny), ((1,), (1,)))
    spec = spec + pltpu.roll(spec, wide - 1, 1)
    slot = lax.broadcasted_iota(jnp.int32, (xy, wide), 1) % 8
    for xx in range(2):
        packed = jnp.zeros((xy, wide), jnp.float32)
        for m in range(M):
            piece = spec[m * xy : (m + 1) * xy, :]
            shift = (m - 2 - 2 * xx) % wide
            piece = pltpu.roll(piece, shift, 1) if shift else piece
            packed = jnp.where(slot == m, piece, packed)
        s1[:, xx : xx + 1, :] = packed.reshape(xy, 1, wide)

    def everyone(axis, size, mine, far, src_of, dst, send, recv, meanwhile=None):
        for i in sorted(range(1, size), key=far, reverse=True):
            to = lax.rem(mine + i, size)
            remote(src_of(to), dst.at[mine], send.at[0], recv.at[0], {axis: to}).start()
        dst[mine] = src_of(mine)[...]
        if meanwhile is not None:
            meanwhile()
        rest = dst.at[pl.ds(0, size - 1)]
        done = remote(rest, rest, send.at[0], recv.at[0], {axis: lax.rem(mine + 1, size)})
        done.wait_recv()
        done.wait_send()

    def hops_xy(i):
        return min(i // 8, 4 - i // 8) + min(i % 8 // 2, 4 - i % 8 // 2)

    def hops_z(i):
        return min(i, gz - i)

    round_of(4)
    everyone("xy", xy, me, hops_xy, lambda to: s1.at[to], r1, a1s, a1r)
    second.start(0)
    second.start(2)
    gathered = jnp.concatenate([r1[:, 0:1, :].reshape(xy, wide), r1[:, 1:2, :].reshape(xy, wide)], axis=0)
    fz[...] = dot3(gathered.T, fx, ((1,), (0,))).reshape(coarse, M, 2 * half)

    up = lax.broadcasted_iota(jnp.int32, (M, 2 * half), 1) < half
    theta = th[...]
    decay = jnp.exp(-theta)
    state = jnp.zeros((M, 2 * half), jnp.float32)
    for t in range(coarse):
        state = decay * state + jnp.where(up, fz[t], fz[coarse - 1 - t])
        wz[t] = state
    ztile[...] = state
    everyone("gz", gz, q, hops_z, lambda to: ztile, zr, gs, gr)
    slab = jnp.exp(-float(coarse) * theta)
    total = jnp.zeros((M, 2 * half), jnp.float32)
    inflow = jnp.zeros((M, 2 * half), jnp.float32)
    steps_in = jnp.where(up, q, gz - 1 - q)
    for t in range(gz):
        inflow = jnp.where(steps_in == t, total, inflow)
        total = slab * total + jnp.where(up, zr[t], zr[gz - 1 - t])
    span = float(coarse * gz + 1)
    image = pltpu.roll(total, half, 1) - jnp.exp(-span * theta) * total
    image = image * jnp.exp(-theta * (float(coarse) * steps_in.astype(jnp.float32) + 1.0))
    inflow = inflow - image / (1.0 - jnp.exp(-2.0 * span * theta))
    scale = 1.0 / (jnp.exp(theta) - decay)
    power = decay
    for t in range(coarse):
        wz[t] = wz[t] + power * inflow
        power = power * decay
    last = decay * wz[coarse - 1]
    beyond = scale * (last + pltpu.roll(inflow, half, 1))
    above, below = jnp.where(has_high, beyond, 0.0), jnp.where(has_low, beyond, 0.0)
    above = pltpu.roll(above, half, 1)
    for z in range(coarse):
        value = scale * (wz[z] + pltpu.roll(wz[coarse - 1 - z], half, 1) - fz[z])
        ring = below if z == 0 else above if z == 1 else 0.0
        vz[pl.ds(z, M, stride=coarse), :] = jnp.where(up, value, ring)
    s2[...] = dot3_table_first(bx, vz[...], ((1,), (1,))).reshape(xy, 8, wide)
    def second_halo():
        second.wait()
        pa[3:top, 0:2, :] = jnp.where(has_near, xqr[1], 0.0)
        pa[3:top, 6:8, :] = jnp.where(has_far, xqr[0], 0.0)
        pa[1:3, 2:6, :] = jnp.where(has_low, zqr[1, :, 2:6, :], 0.0)
        pa[top : top + 2, 2:6, :] = jnp.where(has_high, zqr[0, :, 2:6, :], 0.0)
        for c, (dz, dx) in enumerate(CORNERS):
            z0, z1, x0, x1, there = corner_places(dz, dx)
            pa[z0, x0 : x0 + 1, :] = jnp.where(there, dr[c], 0.0)

        sweep(pa, pb, 1)

        def base_sweep(i, carry):
            pa[i] = relax(pb, i)
            return carry

        lax.fori_loop(3, top, base_sweep, 0, unroll=4)

    everyone("xy", xy, me, hops_xy, lambda to: s2.at[to], r2, a2s, a2r, second_halo)

    block = lax.broadcasted_iota(jnp.int32, (coarse, half * 2), 1) // xy
    for base, deep in ((0, coarse), (4, 8)):
        turned = jnp.concatenate([r2[:, base + e : base + e + 1, :].reshape(xy, wide) for e in range(4)], axis=0).T
        for e in range(4):
            for j in range(2):
                mixed = jnp.zeros((deep, 4 * xy), jnp.float32)
                for b in range(4):
                    at = (4 * j + b) * coarse
                    piece, shift = turned[at : at + deep, :], (b - e) % 4 * xy
                    piece = pltpu.roll(piece, shift, 1) if shift else piece
                    mixed = jnp.where(block[:deep] == b, piece, mixed)
                for twice in range(2):
                    row, count = (2 * e + twice, coarse) if base == 0 else (wide + 2 * e + twice, 2)
                    tm.at[j][pl.ds(row, count, stride=8), :] = mixed[:count]
    fixes = dot3(jnp.concatenate([tm[0], tm[1]], axis=1), ty, ((1,), (0,))).reshape(coarse + 2, 8, ny)
    cc[1 : coarse + 1] = fixes[:coarse]
    cc[0] = fixes[coarse]
    cc[coarse + 1] = fixes[coarse + 1]

    gain = OMEGA / CW

    def shared(z):
        v = cc[z]
        total = v + flat_sum(v)
        return (1.0 - OMEGA) * v + gain * total

    def lifted_sweep(z, carry):
        common = shared(z)
        pb[2 * z + 1] = jnp.where(inside, common + gain * cc[z - 1], 0.0)
        pb[2 * z + 2] = jnp.where(inside, common + gain * cc[z + 1], 0.0)
        return carry

    lax.fori_loop(1, coarse + 1, lifted_sweep, 0, unroll=2)
    pb[2] = jnp.where(jnp.logical_and(inside, has_low), shared(0) + gain * cc[1], 0.0)
    pb[top] = jnp.where(jnp.logical_and(inside, has_high), shared(coarse + 1) + gain * cc[coarse], 0.0)

    def last_sweep(i, carry):
        v, total = neighbours(pb, i)
        potv[i - 3] = (pa[i] + (1.0 - OMEGA) * v + gain * total)[2:6, :]
        return carry

    part = planes // 4
    leaving = []
    for c in range(4):
        lax.fori_loop(3 + c * part, 3 + (c + 1) * part, last_sweep, 0, unroll=4)
        here = pl.ds(c * part, part)
        leaving.append(pltpu.make_async_copy(potv.at[here], out_hbm.at[here], outs.at[c]))
        leaving[-1].start()
    for copy in leaving:
        copy.wait()


def body(gz, xy, consts, source, potential):
    planes, rows, ny = source.shape
    coarse = planes // 2
    wide, two = coarse * 8, 4 * xy
    f32 = jnp.float32
    vm = lambda *shape: pltpu.VMEM(shape, f32)
    half = lambda *shape: pltpu.VMEM((2, *shape), jnp.bfloat16)
    dma = lambda n: pltpu.SemaphoreType.DMA((n,))
    scratch = [
        vm(planes, rows, ny), vm(planes, rows, ny), half(M * xy, ny), half(2 * xy, two), half(8 * xy, two), vm(M, two),
        vm(planes + 6, 8, ny), vm(planes + 6, 8, ny), vm(planes + 4, 8, ny),
        vm(2, planes, 2, ny), vm(2, planes, 2, ny), vm(2, planes, 1, ny), vm(2, planes + 4, 1, ny),
        vm(2, planes, 2, ny), vm(2, planes, 2, ny),
        vm(2, 3, rows, ny), vm(2, 2, rows, ny), vm(4, 4, ny), vm(4, 4, ny),
        vm(2, planes, 2, ny), vm(2, planes, 2, ny), vm(2, 2, 8, ny), vm(4, 1, ny), vm(4, 1, ny),
        vm(coarse, 8, ny), vm(xy, 2, wide), vm(xy, 2, wide), vm(coarse, M, two), vm(coarse, M, two),
        vm(M, two), vm(gz, M, two), vm(wide, two), vm(xy, 8, wide), vm(xy, 8, wide),
        vm(2, wide + 16, 4 * xy), vm(coarse + 2, 8, ny),
        dma(6), dma(14), dma(14), dma(8), dma(8), dma(1), dma(1), dma(1), dma(1), dma(1), dma(1), dma(4),
        pltpu.SemaphoreType.REGULAR((4,)), pltpu.SemaphoreType.REGULAR((4,)),
    ]
    hbm = pl.BlockSpec(memory_space=pl.ANY)
    return pl.pallas_call(
        functools.partial(kernel, gz, xy),
        out_shape=jax.ShapeDtypeStruct(source.shape, f32),
        in_specs=[pl.BlockSpec(memory_space=pltpu.HBM)] * 6,
        out_specs=hbm,
        scratch_shapes=scratch,
        compiler_params=pltpu.CompilerParams(vmem_limit_bytes=24 * 1024 * 1024, collective_id=0, has_side_effects=True),
        name="vcycle",
    )(*[pltpu.with_memory_space_constraint(a, pltpu.HBM) for a in (source, potential, *map(jnp.asarray, consts))])


def solution(mesh):
    gz, xy = mesh.shape["gz"], mesh.shape["xy"]
    consts = tables(xy)
    placed = (P("gz", "xy", None), P("gz", "xy", None))
    return jax.shard_map(
        functools.partial(body, gz, xy, consts), mesh=mesh, in_specs=placed,
        out_specs=P("gz", "xy", None), check_vma=False,
    )
```

```python
import functools
import math

import jax
import jax.numpy as jnp
import ml_dtypes
import numpy as np
from jax import lax
from jax.experimental import pallas as pl
from jax.experimental.pallas import tpu as pltpu
from jax.sharding import PartitionSpec as P

SCREEN = 64
OMEGA = 0.8
KAPPA = 1.0 / (SCREEN * SCREEN)
CW = 6.0 + KAPPA
M = 8
CORNERS = ((-1, -1), (-1, 1), (1, -1), (1, 1))


def sine(count):
    idx = np.arange(1, count + 1, dtype=np.int64)
    turns = idx[:, None] * idx[None, :] % (2 * (count + 1))
    return math.sqrt(2.0 / (count + 1)) * np.sin(math.pi / (count + 1) * turns)


def eigen(count):
    return 2.0 - 2.0 * np.cos(math.pi / (count + 1) * np.arange(1, count + 1))


def two_parts(table):
    coarse = table.astype(ml_dtypes.bfloat16)
    return np.stack([coarse, (table - coarse.astype(np.float64)).astype(ml_dtypes.bfloat16)])


def dot3(value, table, dims):
    coarse = value.astype(jnp.bfloat16)
    fine = (value - coarse.astype(jnp.float32)).astype(jnp.bfloat16)
    dot = lambda a, b: lax.dot_general(a, b, (dims, ((), ())), preferred_element_type=jnp.float32)
    return dot(coarse, table[0]) + dot(fine, table[0]) + dot(coarse, table[1])


def dot3_table_first(table, value, dims):
    coarse = value.astype(jnp.bfloat16)
    fine = (value - coarse.astype(jnp.float32)).astype(jnp.bfloat16)
    dot = lambda a, b: lax.dot_general(a, b, (dims, ((), ())), preferred_element_type=jnp.float32)
    return dot(table[0], coarse) + dot(table[0], fine) + dot(table[1], coarse)


def tables(groups):
    nx, ny = 2 * groups, M * groups
    sx, sy = sine(nx), sine(ny)
    ty = np.repeat(sy, 2, axis=1)
    order = np.concatenate([np.arange(0, nx, 2), np.arange(1, nx, 2)])
    fx = 0.5 * np.concatenate([sx[order], sx[order]], axis=1)
    bx = np.zeros((groups, 8, 2 * nx))
    for d in range(groups):
        for e in range(4):
            x = 2 * d - 1 + e
            if 0 <= x < nx:
                bx[d, e, :nx] = sx[x]
                bx[d, 4 + e, nx:] = sx[x]
    diag = 2.0 + eigen(nx)[None, None, :] + eigen(ny).reshape(M, groups).T[:, :, None] + 4.0 * KAPPA
    theta = np.arccosh(0.5 * diag)
    theta = np.concatenate([theta, theta], axis=2)
    return two_parts(ty), two_parts(fx), two_parts(bx.reshape(groups * 8, 2 * nx)), theta.astype(np.float32)


def kernel(
    gz, xy, src_hbm, pot_hbm, ty_hbm, fx_hbm, bx_hbm, th_hbm, out_hbm,
    potv, srcv, ty, fx, bx, th, pa, pb, sv,
    xps, xpr, xts, xtr, xss, xsr, zpr, zsr, cs, cr,
    xqs, xqr, zqr, ds, dr,
    rs, s1, r1, fz, wz, ztile, zr, vz, s2, r2, tm, cc,
    ld, e1s, e1r, e2s, e2r, a1s, a1r, gs, gr, a2s, a2r, outs, known_x, known_z,
):
    q, me = lax.axis_index("gz"), lax.axis_index("xy")
    planes, rows, ny = potv.shape
    half = 2 * xy
    top = planes + 3

    loads = [
        pltpu.make_async_copy(pot_hbm, potv, ld.at[0]),
        pltpu.make_async_copy(src_hbm, srcv, ld.at[1]),
        pltpu.make_async_copy(ty_hbm, ty, ld.at[2]),
        pltpu.make_async_copy(fx_hbm, fx, ld.at[3]),
        pltpu.make_async_copy(bx_hbm, bx, ld.at[4]),
        pltpu.make_async_copy(th_hbm.at[me], th, ld.at[5]),
    ]
    def shifted(dz, dx):
        where = {}
        if dz:
            where["gz"] = lax.rem(q + dz + gz, gz)
        if dx:
            where["xy"] = lax.rem(me + dx + xy, xy)
        return where

    def tell(sem, where):
        pl.semaphore_signal(sem, inc=1, device_id=where, device_id_type=pl.DeviceIdType.MESH)

    barrier = pltpu.get_barrier_semaphore()
    for dz, dx in CORNERS + ((-1, 0), (1, 0), (0, -1), (0, 1)):
        tell(barrier, shifted(dz, dx))
    loads[0].start()
    loads[1].start()

    for side in range(2):
        xtr[side, 0:2] = jnp.zeros((2, 1, ny), jnp.float32)
        xtr[side, planes + 2 : planes + 4] = jnp.zeros((2, 1, ny), jnp.float32)
    loads[0].wait()
    xps[0] = potv[:, 0:2, :]
    xps[1] = potv[:, 2:4, :]
    xts[0] = potv[:, 2:3, :]
    xts[1] = potv[:, 1:2, :]
    pl.semaphore_wait(barrier, 8)

    def round_of(level):
        for axis, size, dim, known in (("xy", xy, 1, known_x), ("gz", gz, 0, known_z)):
            reach = 2**level
            if level and reach // 2 < size // 2:
                pl.semaphore_wait(known.at[level - 1], 2)
            if reach < size // 2:
                for way in (-reach, reach):
                    tell(known.at[level], shifted(way, 0) if dim == 0 else shifted(0, way))

    class Exchange:
        def __init__(self, send, recv):
            self.send, self.recv, self.copies = send, recv, []

        def add(self, src, dst, dz, dx):
            slot = len(self.copies)
            copy = remote(src, dst, self.send.at[slot], self.recv.at[slot], shifted(dz, dx))
            self.copies.append((copy, exists(dz, dx), exists(-dz, -dx)))

        def start(self, slot):
            copy, there, unused = self.copies[slot]
            pl.when(there)(copy.start)

        def wait(self):
            for copy, there, back in self.copies:
                pl.when(back)(copy.wait_recv)
                pl.when(there)(copy.wait_send)

    def exists(dz, dx):
        there = None
        for step, mine, size in ((dz, q, gz), (dx, me, xy)):
            if step:
                ok = mine > 0 if step < 0 else mine < size - 1
                there = ok if there is None else jnp.logical_and(there, ok)
        return there

    def remote(src, dst, send, recv, where):
        return pltpu.make_async_remote_copy(
            src_ref=src, dst_ref=dst, send_sem=send, recv_sem=recv,
            device_id=where, device_id_type=pl.DeviceIdType.MESH,
        )

    first = Exchange(e1s, e1r)
    for side, step in ((0, -1), (1, 1)):
        first.add(xps.at[side], xpr.at[side], 0, step)
        first.add(xts.at[side], xtr.at[side, pl.ds(2, planes)], 0, step)
        first.add(xss.at[side], xsr.at[side], 0, step)
        first.add(potv.at[pl.ds(0 if step < 0 else planes - 3, 3)], zpr.at[side], step, 0)
        first.add(srcv.at[pl.ds(0 if step < 0 else planes - 2, 2)], zsr.at[side], step, 0)
    for c, (dz, dx) in enumerate(CORNERS):
        first.add(cs.at[c], cr.at[c], dz, dx)
    for slot in (0, 5, 1, 6, 3, 8):
        first.start(slot)
    round_of(0)
    loads[1].wait()
    xss[0] = srcv[:, 0:2, :]
    xss[1] = srcv[:, 2:4, :]
    for c, (dz, dx) in enumerate(CORNERS):
        z0, z1 = (0, 1) if dz < 0 else (planes - 1, planes - 2)
        x0, x1 = (0, 1) if dx < 0 else (rows - 1, rows - 2)
        cs[c, 0:1] = potv[z0, x0 : x0 + 1, :]
        cs[c, 1:2] = potv[z0, x1 : x1 + 1, :]
        cs[c, 2:3] = potv[z1, x0 : x0 + 1, :]
        cs[c, 3:4] = srcv[z0, x0 : x0 + 1, :]
    for slot in (2, 7, 4, 9, 10, 11, 12, 13):
        first.start(slot)
    for copy in loads[2:]:
        copy.start()

    pa[...] = jnp.zeros_like(pa)
    sv[...] = jnp.zeros_like(sv)
    pa[3:top, 2:6, :] = potv[...]
    sv[2 : planes + 2, 2:6, :] = srcv[...]
    sub = lax.broadcasted_iota(jnp.int32, (8, ny), 0)
    lane = lax.broadcasted_iota(jnp.int32, (8, ny), 1)
    inside = jnp.logical_and(
        jnp.logical_or(sub >= 2, me > 0), jnp.logical_or(sub < 6, me < xy - 1)
    )
    has_low, has_high, has_near, has_far = q > 0, q < gz - 1, me > 0, me < xy - 1

    def corner_places(dz, dx):
        z0, z1 = (top, top + 1) if dz < 0 else (2, 1)
        x0, x1 = (6, 7) if dx < 0 else (1, 0)
        return z0, z1, x0, x1, exists(-dz, -dx)

    round_of(1)
    round_of(2)
    first.wait()
    pa[3:top, 0:2, :] = jnp.where(has_near, xpr[1], 0.0)
    pa[3:top, 6:8, :] = jnp.where(has_far, xpr[0], 0.0)
    pa[0:3, 2:6, :] = jnp.where(has_low, zpr[1], 0.0)
    pa[top : top + 3, 2:6, :] = jnp.where(has_high, zpr[0], 0.0)
    sv[2 : planes + 2, 0:2, :] = jnp.where(has_near, xsr[1], 0.0)
    sv[2 : planes + 2, 6:8, :] = jnp.where(has_far, xsr[0], 0.0)
    sv[0:2, 2:6, :] = jnp.where(has_low, zsr[1], 0.0)
    sv[planes + 2 : planes + 4, 2:6, :] = jnp.where(has_high, zsr[0], 0.0)
    for c, (dz, dx) in enumerate(CORNERS):
        z0, z1, x0, x1, there = corner_places(dz, dx)
        corner = jnp.where(there, cr[c], 0.0)
        pa[z0, x0 : x0 + 1, :] = corner[0:1]
        pa[z0, x1 : x1 + 1, :] = corner[1:2]
        pa[z1, x0 : x0 + 1, :] = corner[2:3]
        sv[z0 - 1, x0 : x0 + 1, :] = corner[3:4]

    def row_sum(v):
        before = jnp.where(lane == 0, 0.0, pltpu.roll(v, 1, 1))
        return before + jnp.where(lane == ny - 1, 0.0, pltpu.roll(v, ny - 1, 1))

    def flat_sum(v):
        return pltpu.roll(v, 1, 0) + pltpu.roll(v, 7, 0) + row_sum(v)

    def neighbours(ref, i, ends=None):
        v = ref[i]
        total = ref[i - 1] + ref[i + 1]
        back, forth = pltpu.roll(v, 1, 0), pltpu.roll(v, 7, 0)
        if ends is not None:
            back, forth = jnp.where(sub == 0, ends[0], back), jnp.where(sub == 7, ends[1], forth)
        return v, total + back + forth + row_sum(v)

    def relax(ref, i, ends=None):
        v, total = neighbours(ref, i, ends)
        return (1.0 - OMEGA) * v + (OMEGA / CW) * (sv[i - 1] + total)

    def sweep(src, dst, ring, ended=False):
        def step(i, carry):
            ends = None
            if ended:
                ends = [jnp.where(there, xtr[side, i - 1], 0.0) for there, side in ((has_near, 1), (has_far, 0))]
            dst[i] = jnp.where(inside, relax(src, i, ends), 0.0)
            return carry

        if ring == 2:
            lax.fori_loop(1, top + 2, step, 0, unroll=4)
        else:
            lax.fori_loop(3, top, step, 0, unroll=4)
            step(2, 0)
            step(top, 0)
        for i in range(ring):
            dst[2 - i] = jnp.where(has_low, dst[2 - i], 0.0)
            dst[top + i] = jnp.where(has_high, dst[top + i], 0.0)

    sweep(pa, pb, 2, True)

    sweep(pb, pa, 1)
    round_of(3)

    xqs[0] = pa[3:top, 2:4, :]
    xqs[1] = pa[3:top, 4:6, :]
    for c, (dz, dx) in enumerate(CORNERS):
        z, x = 3 if dz < 0 else top - 1, 2 if dx < 0 else 5
        ds[c] = pa[z, x : x + 1, :]
    second = Exchange(e2s, e2r)
    for side, step in ((0, -1), (1, 1)):
        second.add(xqs.at[side], xqr.at[side], 0, step)
        second.add(pa.at[pl.ds(3 if step < 0 else top - 2, 2)], zqr.at[side], step, 0)
    for c, (dz, dx) in enumerate(CORNERS):
        second.add(ds.at[c], dr.at[c], dz, dx)
    for slot in (1, 3, 4, 5, 6, 7):
        second.start(slot)

    def residual(i):
        v, total = neighbours(pa, i)
        return sv[i - 1] - CW * v + total

    def coarsen(z, carry):
        rs[z] = residual(2 * z + 3) + residual(2 * z + 4)
        return carry

    coarse = planes // 2
    lax.fori_loop(0, coarse, coarsen, 0, unroll=2)
    for copy in loads[2:]:
        copy.wait()
    wide = coarse * 8
    spec = dot3_table_first(ty, rs[...].reshape(wide, ny), ((1,), (1,)))
    spec = spec + pltpu.roll(spec, wide - 1, 1)
    slot = lax.broadcasted_iota(jnp.int32, (xy, wide), 1) % 8
    for xx in range(2):
        packed = jnp.zeros((xy, wide), jnp.float32)
        for m in range(M):
            piece = spec[m * xy : (m + 1) * xy, :]
            shift = (m - 2 - 2 * xx) % wide
            piece = pltpu.roll(piece, shift, 1) if shift else piece
            packed = jnp.where(slot == m, piece, packed)
        s1[:, xx : xx + 1, :] = packed.reshape(xy, 1, wide)

    def everyone(axis, size, mine, far, src_of, dst, send, recv, meanwhile=None):
        for i in sorted(range(1, size), key=far, reverse=True):
            to = lax.rem(mine + i, size)
            remote(src_of(to), dst.at[mine], send.at[0], recv.at[0], {axis: to}).start()
        dst[mine] = src_of(mine)[...]
        if meanwhile is not None:
            meanwhile()
        rest = dst.at[pl.ds(0, size - 1)]
        done = remote(rest, rest, send.at[0], recv.at[0], {axis: lax.rem(mine + 1, size)})
        done.wait_recv()
        done.wait_send()

    def hops_xy(i):
        return min(i // 8, 4 - i // 8) + min(i % 8 // 2, 4 - i % 8 // 2)

    def hops_z(i):
        return min(i, gz - i)

    round_of(4)
    everyone("xy", xy, me, hops_xy, lambda to: s1.at[to], r1, a1s, a1r)
    second.start(0)
    second.start(2)
    gathered = jnp.concatenate([r1[:, 0:1, :].reshape(xy, wide), r1[:, 1:2, :].reshape(xy, wide)], axis=0)
    fz[...] = dot3(gathered.T, fx, ((1,), (0,))).reshape(coarse, M, 2 * half)

    up = lax.broadcasted_iota(jnp.int32, (M, 2 * half), 1) < half
    theta = th[...]
    decay = jnp.exp(-theta)
    state = jnp.zeros((M, 2 * half), jnp.float32)
    for t in range(coarse):
        state = decay * state + jnp.where(up, fz[t], fz[coarse - 1 - t])
        wz[t] = state
    ztile[...] = state
    everyone("gz", gz, q, hops_z, lambda to: ztile, zr, gs, gr)
    slab = jnp.exp(-float(coarse) * theta)
    total = jnp.zeros((M, 2 * half), jnp.float32)
    inflow = jnp.zeros((M, 2 * half), jnp.float32)
    steps_in = jnp.where(up, q, gz - 1 - q)
    for t in range(gz):
        inflow = jnp.where(steps_in == t, total, inflow)
        total = slab * total + jnp.where(up, zr[t], zr[gz - 1 - t])
    span = float(coarse * gz + 1)
    image = pltpu.roll(total, half, 1) - jnp.exp(-span * theta) * total
    image = image * jnp.exp(-theta * (float(coarse) * steps_in.astype(jnp.float32) + 1.0))
    inflow = inflow - image / (1.0 - jnp.exp(-2.0 * span * theta))
    scale = 1.0 / (jnp.exp(theta) - decay)
    power = decay
    for t in range(coarse):
        wz[t] = wz[t] + power * inflow
        power = power * decay
    last = decay * wz[coarse - 1]
    beyond = scale * (last + pltpu.roll(inflow, half, 1))
    above, below = jnp.where(has_high, beyond, 0.0), jnp.where(has_low, beyond, 0.0)
    above = pltpu.roll(above, half, 1)
    for z in range(coarse):
        value = scale * (wz[z] + pltpu.roll(wz[coarse - 1 - z], half, 1) - fz[z])
        ring = below if z == 0 else above if z == 1 else 0.0
        vz[pl.ds(z, M, stride=coarse), :] = jnp.where(up, value, ring)
    s2[...] = dot3_table_first(bx, vz[...], ((1,), (1,))).reshape(xy, 8, wide)
    def second_halo():
        second.wait()
        pa[3:top, 0:2, :] = jnp.where(has_near, xqr[1], 0.0)
        pa[3:top, 6:8, :] = jnp.where(has_far, xqr[0], 0.0)
        pa[1:3, 2:6, :] = jnp.where(has_low, zqr[1, :, 2:6, :], 0.0)
        pa[top : top + 2, 2:6, :] = jnp.where(has_high, zqr[0, :, 2:6, :], 0.0)
        for c, (dz, dx) in enumerate(CORNERS):
            z0, z1, x0, x1, there = corner_places(dz, dx)
            pa[z0, x0 : x0 + 1, :] = jnp.where(there, dr[c], 0.0)

        sweep(pa, pb, 1)

        def base_sweep(i, carry):
            pa[i] = relax(pb, i)
            return carry

        lax.fori_loop(3, top, base_sweep, 0, unroll=4)

    everyone("xy", xy, me, hops_xy, lambda to: s2.at[to], r2, a2s, a2r, second_halo)

    block = lax.broadcasted_iota(jnp.int32, (coarse, half * 2), 1) // xy
    for base, deep in ((0, coarse), (4, 8)):
        turned = jnp.concatenate([r2[:, base + e : base + e + 1, :].reshape(xy, wide) for e in range(4)], axis=0).T
        for e in range(4):
            for j in range(2):
                mixed = jnp.zeros((deep, 4 * xy), jnp.float32)
                for b in range(4):
                    at = (4 * j + b) * coarse
                    piece, shift = turned[at : at + deep, :], (b - e) % 4 * xy
                    piece = pltpu.roll(piece, shift, 1) if shift else piece
                    mixed = jnp.where(block[:deep] == b, piece, mixed)
                for twice in range(2):
                    row, count = (2 * e + twice, coarse) if base == 0 else (wide + 2 * e + twice, 2)
                    tm.at[j][pl.ds(row, count, stride=8), :] = mixed[:count]
    fixes = dot3(jnp.concatenate([tm[0], tm[1]], axis=1), ty, ((1,), (0,))).reshape(coarse + 2, 8, ny)
    cc[1 : coarse + 1] = fixes[:coarse]
    cc[0] = fixes[coarse]
    cc[coarse + 1] = fixes[coarse + 1]

    gain = OMEGA / CW

    def shared(z):
        v = cc[z]
        total = v + flat_sum(v)
        return (1.0 - OMEGA) * v + gain * total

    def lifted_sweep(z, carry):
        common = shared(z)
        pb[2 * z + 1] = jnp.where(inside, common + gain * cc[z - 1], 0.0)
        pb[2 * z + 2] = jnp.where(inside, common + gain * cc[z + 1], 0.0)
        return carry

    lax.fori_loop(1, coarse + 1, lifted_sweep, 0, unroll=2)
    pb[2] = jnp.where(jnp.logical_and(inside, has_low), shared(0) + gain * cc[1], 0.0)
    pb[top] = jnp.where(jnp.logical_and(inside, has_high), shared(coarse + 1) + gain * cc[coarse], 0.0)

    def last_sweep(i, carry):
        v, total = neighbours(pb, i)
        potv[i - 3] = (pa[i] + (1.0 - OMEGA) * v + gain * total)[2:6, :]
        return carry

    part = planes // 4
    leaving = []
    for c in range(4):
        lax.fori_loop(3 + c * part, 3 + (c + 1) * part, last_sweep, 0, unroll=4)
        here = pl.ds(c * part, part)
        leaving.append(pltpu.make_async_copy(potv.at[here], out_hbm.at[here], outs.at[c]))
        leaving[-1].start()
    for copy in leaving:
        copy.wait()


def body(gz, xy, consts, source, potential):
    planes, rows, ny = source.shape
    coarse = planes // 2
    wide, two = coarse * 8, 4 * xy
    f32 = jnp.float32
    vm = lambda *shape: pltpu.VMEM(shape, f32)
    half = lambda *shape: pltpu.VMEM((2, *shape), jnp.bfloat16)
    dma = lambda n: pltpu.SemaphoreType.DMA((n,))
    scratch = [
        vm(planes, rows, ny), vm(planes, rows, ny), half(M * xy, ny), half(2 * xy, two), half(8 * xy, two), vm(M, two),
        vm(planes + 6, 8, ny), vm(planes + 6, 8, ny), vm(planes + 4, 8, ny),
        vm(2, planes, 2, ny), vm(2, planes, 2, ny), vm(2, planes, 1, ny), vm(2, planes + 4, 1, ny),
        vm(2, planes, 2, ny), vm(2, planes, 2, ny),
        vm(2, 3, rows, ny), vm(2, 2, rows, ny), vm(4, 4, ny), vm(4, 4, ny),
        vm(2, planes, 2, ny), vm(2, planes, 2, ny), vm(2, 2, 8, ny), vm(4, 1, ny), vm(4, 1, ny),
        vm(coarse, 8, ny), vm(xy, 2, wide), vm(xy, 2, wide), vm(coarse, M, two), vm(coarse, M, two),
        vm(M, two), vm(gz, M, two), vm(wide, two), vm(xy, 8, wide), vm(xy, 8, wide),
        vm(2, wide + 16, 4 * xy), vm(coarse + 2, 8, ny),
        dma(6), dma(14), dma(14), dma(8), dma(8), dma(1), dma(1), dma(1), dma(1), dma(1), dma(1), dma(4),
        pltpu.SemaphoreType.REGULAR((4,)), pltpu.SemaphoreType.REGULAR((4,)),
    ]
    hbm = pl.BlockSpec(memory_space=pl.ANY)
    return pl.pallas_call(
        functools.partial(kernel, gz, xy),
        out_shape=jax.ShapeDtypeStruct(source.shape, f32),
        in_specs=[pl.BlockSpec(memory_space=pltpu.HBM)] * 6,
        out_specs=hbm,
        scratch_shapes=scratch,
        compiler_params=pltpu.CompilerParams(vmem_limit_bytes=24 * 1024 * 1024, collective_id=0, has_side_effects=True),
        name="vcycle",
    )(*[pltpu.with_memory_space_constraint(a, pltpu.HBM) for a in (source, potential, *map(jnp.asarray, consts))])


def solution(mesh):
    gz, xy = mesh.shape["gz"], mesh.shape["xy"]
    consts = tables(xy)
    placed = (P("gz", "xy", None), P("gz", "xy", None))
    return jax.shard_map(
        functools.partial(body, gz, xy, consts), mesh=mesh, in_specs=placed,
        out_specs=P("gz", "xy", None), check_vma=False,
    )
```
